32 devices in a mesh: vec: 8 (over y, x, core), row: 4 (over z).
Axes of the slice: x: 2, y: 2, z: 4, core: 2. Of those that a mesh axis runs over, the one named last changes fastest.
Arguments:
- vectors: float32 [512, 131072], P('vec', 'row'), may hold values from -6 to 6
- col_blocks: int32 [1024, 16], P('row'), may hold values from 0 to 1023, as said below
- op_ids: int32 [1024, 16], P('row'), may hold values from 0 to 15
- coefficients: float32 [1024, 16], P('row'), may hold values from -6 to 6
- onsite: float32 [131072], P('row'), may hold values from -0.5 to 3
- phonon_ops: float32 [16, 128, 128], replicated, may hold values from -0.125 to 0.125
Outputs:
- filtered: float32 [512, 131072], P('vec', 'row')
The draws below stay inside these ranges and needn't reach their ends.
Inputs may be any that keep to these rules, and one draw needn't show every extreme that they name: `col_blocks`: entry j of block row b lies within 8 of b; entry 0 is b + 8 for even b and b - 8 for odd b, clipped to the 1024 blocks.
All inputs are finite; a program needn't handle non-finite values.
Results may differ from the reference program's by a relative error of at most 0.0003.
Values sent between devices are 32-bit elements; how exact they have to be, the bound alone decides.
No kernel may reach another device: no remote copies, remote signals or barrier semaphores. Data moves between devices by JAX's collectives and lax.ppermute only.
A program may use at most 128 MiB of HBM per device.

```python
import math
import jax
import jax.numpy as jnp
from jax import lax

ROWS = 131072
VECS = 512
BS = 128
NOPS = 16
NNZB = 16
BAND = 8
NS_ITERS = 3
NBLK = 1024


def draw_col_blocks(key, part):
    offsets = jax.random.randint(key, (NBLK, NNZB), -BAND, BAND + 1).astype(jnp.int32)
    block_rows = jnp.arange(NBLK, dtype=jnp.int32)[:, None]
    leading = jnp.where(block_rows % 2 == 0, BAND, -BAND).astype(jnp.int32)
    offsets = jnp.concatenate([leading, offsets[:, 1:]], axis=1)
    return jnp.clip(block_rows + offsets, 0, NBLK - 1).astype(jnp.int32)


def draw_onsite(key, part):
    position = jnp.arange(ROWS, dtype=jnp.float32) / ROWS
    noise = jax.random.uniform(key, (ROWS,), jnp.float32, -0.5, 0.5)
    return (2.5 * position + noise).astype(jnp.float32)


def with_ends(result, stream_key, smallest, largest):
    longest = result.shape.index(max(result.shape))
    spots = []
    for shift in (0, 1):
        where = [jax.random.randint(jax.random.fold_in(stream_key, axis), (), 0, length) for axis, length in enumerate(result.shape)]
        where[longest] = (where[longest] + shift) % result.shape[longest]
        spots.append(tuple(where))
    return result.at[spots[0]].set(smallest).at[spots[1]].set(largest)


def block_levels(key, shape, split, low, largest):
    def one(dim, parts):
        heights = jax.random.uniform(jax.random.fold_in(jax.random.fold_in(key, 6), dim), (parts,), jnp.float32, low / len(split), largest / len(split))
        return jnp.repeat(jnp.exp(heights), shape[dim] // parts).reshape((-1,) + (1,) * (len(shape) - dim - 1))

    factor_of = one(*split[0])
    for cut in split[1:]:
        factor_of = factor_of * one(*cut)
    return factor_of


def scatter_about(own_key, extent, width, bound, pieces=(), kind=jnp.bfloat16):
    result = jax.random.normal(own_key, extent, jnp.float32) * width
    if len(pieces) > 0:
        result = block_levels(own_key, extent, pieces, -0.22, 0.18) * result
    return jnp.clip(result, min=-bound, max=bound).astype(kind)


def setup_inputs(seed: int = 0) -> dict:
    arg_keys = jax.random.split(jax.random.key(seed), 7)
    vectors = scatter_about(arg_keys[0], (VECS, ROWS), 1.0, 6.0, ((0, 8), (1, 4)), jnp.float32)
    col_blocks = draw_col_blocks(jax.random.fold_in(arg_keys[6], 71), 0)
    op_ids = with_ends(jax.random.randint(arg_keys[2], (NBLK, NNZB), 0, NOPS), jax.random.fold_in(arg_keys[2], 1), 0, NOPS - 1).astype(jnp.int32)
    coefficients = scatter_about(arg_keys[3], (NBLK, NNZB), 1.0, 6.0, ((0, 4),), jnp.float32)
    onsite = draw_onsite(jax.random.fold_in(arg_keys[6], 71), 0)
    phonon_ops = scatter_about(arg_keys[5], (NOPS, BS, BS), (NNZB * BS) ** -0.5, 0.125, (), jnp.float32)
    return {"vectors": vectors, "col_blocks": col_blocks, "op_ids": op_ids, "coefficients": coefficients, "onsite": onsite, "phonon_ops": phonon_ops}


CENTER = 0.25
HALF_WIDTH = 2.0
EPSILON = 1e-06
HIGH = lax.Precision.HIGHEST

def apply_ham(source, onsite, col_blocks, op_ids, coefficients, phonon_ops):
    vec_count, row_count = source.shape
    blocks = source.reshape(vec_count, NBLK, BS)
    w_op = jnp.transpose(phonon_ops, (0, 2, 1))
    op_range = jnp.arange(NOPS, dtype=jnp.int32)
    weight_all = (op_ids[:, :, None] == op_range[None, None, :]).astype(jnp.float32) * coefficients[:, :, None]
    group_rows = math.gcd(NBLK, 32)

    def one_group(index):
        block_index = lax.dynamic_slice_in_dim(col_blocks, index * group_rows, group_rows, 0)
        weight_rows = lax.dynamic_slice_in_dim(weight_all, index * group_rows, group_rows, 0)
        picked = jnp.take(blocks, block_index, axis=1)
        mixture = jnp.einsum('vbjs,bjo->bovs', picked, weight_rows, precision=HIGH)
        return lax.dot_general(mixture, w_op, (((1, 3), (0, 1)), ((), ())), precision=HIGH)
    results = lax.map(one_group, jnp.arange(NBLK // group_rows, dtype=jnp.int32))
    coupled = results.reshape(NBLK, vec_count, BS).transpose(1, 0, 2).reshape(vec_count, row_count)
    return onsite[None, :] * source + coupled

def reference(vectors, col_blocks, op_ids, coefficients, onsite, phonon_ops):
    first_step = (apply_ham(vectors, onsite, col_blocks, op_ids, coefficients, phonon_ops) - CENTER * vectors) / HALF_WIDTH
    second_step = 2.0 * (apply_ham(first_step, onsite, col_blocks, op_ids, coefficients, phonon_ops) - CENTER * first_step) / HALF_WIDTH - vectors
    gram = lax.dot_general(second_step, second_step, (((1,), (1,)), ((), ())), precision=HIGH)
    gram_norm = jnp.sqrt(jnp.sum(gram * gram) + EPSILON)
    identity = jnp.eye(VECS, dtype=jnp.float32)
    approx = gram / gram_norm
    inverse = identity
    for step in range(NS_ITERS):
        correction = (3.0 * identity - jnp.dot(inverse, approx, precision=HIGH)) / 2.0
        if step + 1 < NS_ITERS:
            approx = jnp.dot(approx, correction, precision=HIGH)
        inverse = jnp.dot(correction, inverse, precision=HIGH)
    rotated = lax.dot_general(inverse, second_step, (((0,), (0,)), ((), ())), precision=HIGH)
    return rotated * jnp.sqrt(ROWS / gram_norm)
```

```python
import functools

import jax
import jax.numpy as jnp
from jax import lax
from jax.experimental import pallas as pl
from jax.experimental.pallas import tpu as pltpu
from jax.sharding import PartitionSpec as P

BAND = 8
NS_ITERS = 3
CENTER = 0.25
HALF_WIDTH = 2.0
EPSILON = 1e-06
LANES = 128
RING = 3
VMEM_LIMIT = 58 * 1024 * 1024


def split(x):
    hi = x.astype(jnp.bfloat16)
    lo = (x - hi.astype(jnp.float32)).astype(jnp.bfloat16)
    return hi, lo


def dot(a, b):
    return jnp.dot(a, b, preferred_element_type=jnp.float32)


def ham_kernel(
    me_ref, idx_ref, coef_ref, *refs, steps, row_base, ring_base, op_count, per_row, has_low, has_high, second, parts, part_blocks
):
    refs = list(refs)
    main_ref = refs.pop(0)
    low_ref = refs.pop(0) if has_low else None
    high_ref = refs.pop(0) if has_high else None
    onsite_ref = refs.pop(0)
    base_ref = refs.pop(0) if second else None
    w_ref = refs.pop(0)
    outs = [refs.pop(0) for _ in range(parts if second else 1)]
    ring_ref = refs.pop(0)
    self_ref = refs.pop(0)
    stage_ref = refs.pop(0) if second else None
    i = pl.program_id(0)
    vec_count = main_ref.shape[0]
    source = main_ref[...]
    if has_low:
        source = jnp.where(i < 2, low_ref[...], source)
    if has_high:
        source = jnp.where(i >= steps - 2, high_ref[...], source)
    slot = lax.rem(i + ring_base, RING) * (BAND * op_count)
    x = jnp.concatenate([source[:, g * LANES : (g + 1) * LANES] for g in range(BAND)], axis=0)
    hi, lo = split(x)
    lhs = jnp.concatenate([hi, lo, hi], axis=1)
    for o in range(0, op_count, 2):
        t = dot(lhs, w_ref[:, o * LANES : (o + 2) * LANES])
        for g in range(BAND):
            for k in range(2):
                ring_ref[slot + g * op_count + o + k] = t[
                    g * vec_count : (g + 1) * vec_count, k * LANES : (k + 1) * LANES
                ]

    @pl.when(i >= 2)
    def _():
        previous = lax.rem(i + 1, 2)
        for g in range(BAND):
            block = (i - 2) * BAND + g
            row = (block + row_base) * per_row
            span = slice(g * LANES, (g + 1) * LANES)
            own = self_ref[previous, :, span]
            acc = (onsite_ref[:, span] - CENTER) * own
            for j in range(per_row):
                acc = acc + coef_ref[row + j] * ring_ref[idx_ref[row + j]]
            if second:
                acc = acc - base_ref[:, span]
                peer = lax.div(block, part_blocks)
                place = jnp.bitwise_xor(peer, me_ref[0]) * part_blocks + lax.rem(block, part_blocks)
                stage_ref[place] = acc
            else:
                outs[0][:, span] = acc * (1.0 / HALF_WIDTH)

    self_ref[lax.rem(i, 2)] = source
    if second:

        @pl.when(i == steps - 1)
        def _():
            for part in range(parts):
                for s in range(part_blocks):
                    outs[part][:, s * LANES : (s + 1) * LANES] = stage_ref[part * part_blocks + s]


def apply_ham(
    me, idx, coef, onsite, w, main, main_chunk, chunks, row_chunk, ring_base, onsite_chunk,
    low=None, low_chunk=0, high=None, high_chunk=0, base=None, base_chunk=0, parts=0, part_blocks=1, op_count=16, per_row=16,
):
    vec_count = main.shape[0]
    width = BAND * LANES
    steps = chunks + 2
    second = base is not None
    main_first = 2 if low is not None else 0
    main_last = steps - 1 - (2 if high is not None else 0)
    spec = functools.partial(pl.BlockSpec, (vec_count, width))
    in_specs = [spec(lambda i, *_: (0, jnp.clip(i, main_first, main_last) - main_first + main_chunk))]
    args = [main]
    if low is not None:
        in_specs.append(spec(lambda i, *_: (0, jnp.clip(i, 0, 1) + low_chunk)))
        args.append(low)
    if high is not None:
        in_specs.append(spec(lambda i, *_: (0, jnp.clip(i - (steps - 2), 0, 1) + high_chunk)))
        args.append(high)
    in_specs.append(pl.BlockSpec((1, width), lambda i, *_: (0, jnp.maximum(i - 2, 0) + onsite_chunk)))
    args.append(onsite)
    if second:
        in_specs.append(spec(lambda i, *_: (0, jnp.maximum(i - 2, 0) + base_chunk)))
        args.append(base)
    in_specs.append(pl.BlockSpec(w.shape, lambda i, *_: (0, 0)))
    args.append(w)
    scratch = [
        pltpu.VMEM((RING * BAND * op_count, vec_count, LANES), jnp.float32),
        pltpu.VMEM((2, vec_count, width), jnp.float32),
    ]
    if second:
        out_shape = [jax.ShapeDtypeStruct((vec_count, part_blocks * LANES), jnp.float32)] * parts
        out_specs = [pl.BlockSpec((vec_count, part_blocks * LANES), lambda i, *_: (0, 0))] * parts
        scratch.append(pltpu.VMEM((parts * part_blocks, vec_count, LANES), jnp.float32))
    else:
        out_shape = [jax.ShapeDtypeStruct((vec_count, chunks * width), jnp.float32)]
        out_specs = [spec(lambda i, *_: (0, jnp.maximum(i - 2, 0)))]
    flops = 2 * steps * BAND * vec_count * 3 * LANES * LANES * op_count
    return pl.pallas_call(
        functools.partial(
            ham_kernel,
            steps=steps,
            row_base=row_chunk * BAND,
            ring_base=ring_base,
            op_count=op_count,
            per_row=per_row,
            has_low=low is not None,
            has_high=high is not None,
            second=second,
            parts=parts,
            part_blocks=part_blocks,
        ),
        out_shape=out_shape,
        grid_spec=pltpu.PrefetchScalarGridSpec(
            num_scalar_prefetch=3, grid=(steps,), in_specs=in_specs, out_specs=out_specs, scratch_shapes=scratch
        ),
        compiler_params=pltpu.CompilerParams(vmem_limit_bytes=VMEM_LIMIT),
        cost_estimate=pl.CostEstimate(flops=2 * flops, transcendentals=0, bytes_accessed=8 * steps * vec_count * width),
        name="ham_second" if second else "ham_first",
    )(me, idx, coef, *args)


def gram_kernel(me_ref, *refs, parts, first, last):
    refs = list(refs)
    pieces = [refs.pop(0) for _ in range(parts)]
    before_ref = None if first else refs.pop(0)
    hi_ref, lo_ref = refs.pop(0), refs.pop(0)
    outs = [refs.pop(0) for _ in range(parts if last else 1)]
    stage_ref = refs.pop(0)
    me = me_ref[0]
    vec_count = pieces[0].shape[0]
    total = parts * vec_count
    for t in range(parts):
        place = pl.multiple_of(jnp.bitwise_xor(me, t) * vec_count, vec_count)
        hi, lo = split(pieces[t][...])
        hi_ref[pl.ds(place, vec_count), :] = hi
        lo_ref[pl.ds(place, vec_count), :] = lo
    contract = (((1,), (1,)), ((), ()))
    hi, lo = hi_ref[...], lo_ref[...]
    square = lax.dot_general(hi, hi, contract, preferred_element_type=jnp.float32)
    cross = lax.dot_general(hi, lo, contract, preferred_element_type=jnp.float32)
    if first:
        stage_ref[0] = square
        stage_ref[1] = cross
    else:
        stage_ref[0] = before_ref[0] + square
        stage_ref[1] = before_ref[1] + cross
    if not last:
        outs[0][...] = stage_ref[...]
    else:
        packed_ref = refs.pop(0)
        tile = total // 4
        at = 0
        for left in range(4):
            for right in range(left, 4):
                a = slice(left * tile, (left + 1) * tile)
                b = slice(right * tile, (right + 1) * tile)
                packed_ref[at * tile : (at + 1) * tile, :] = (
                    stage_ref[0, a, b] + stage_ref[1, a, b] + stage_ref[1, b, a].T
                )
                at += 1
        rows = at * tile // parts
        for t in range(parts):
            place = pl.multiple_of(jnp.bitwise_xor(me, t) * rows, 8)
            outs[t][...] = packed_ref[pl.ds(place, rows), :]


def gram_step(me, pieces, before, last):
    parts = len(pieces)
    vec_count, length = pieces[0].shape
    total = parts * vec_count
    whole = jax.ShapeDtypeStruct((total, length), jnp.bfloat16)
    tile = total // 4
    if last:
        outs = [jax.ShapeDtypeStruct((10 * tile // parts, tile), jnp.float32)] * parts
        extra = [pltpu.VMEM((10 * tile, tile), jnp.float32)]
    else:
        outs = [jax.ShapeDtypeStruct((2, total, total), jnp.float32)]
        extra = []
    vmem = pl.BlockSpec(memory_space=pltpu.VMEM)
    args = list(pieces) + ([] if before is None else [before])
    return pl.pallas_call(
        functools.partial(gram_kernel, parts=parts, first=before is None, last=last),
        out_shape=[whole, whole] + outs,
        in_specs=[pl.BlockSpec(memory_space=pltpu.SMEM)] + [vmem] * len(args),
        out_specs=[vmem] * (2 + len(outs)),
        scratch_shapes=[pltpu.VMEM((2, total, total), jnp.float32)] + extra,
        compiler_params=pltpu.CompilerParams(vmem_limit_bytes=VMEM_LIMIT),
        cost_estimate=pl.CostEstimate(
            flops=4 * total * total * length, transcendentals=0, bytes_accessed=8 * total * length
        ),
        name="gram_step",
    )(me, *args)


def sum_kernel(*refs):
    acc = refs[0][...]
    for ref in refs[1:-1]:
        acc = acc + ref[...]
    refs[-1][...] = acc


def sum_of(arrays):
    return pl.pallas_call(
        sum_kernel, out_shape=jax.ShapeDtypeStruct(arrays[0].shape, jnp.float32), name="sum_of"
    )(*arrays)


def inverse_kernel(me_ref, *refs, parts, total, scale_rows):
    pieces = refs[:parts]
    hi_ref, lo_ref, packed_ref, gram_ref = refs[parts:]
    me = me_ref[0]
    rows = pieces[0].shape[0]
    for t in range(parts):
        place = pl.multiple_of(jnp.bitwise_xor(me, t) * rows, 8)
        packed_ref[pl.ds(place, rows), :] = pieces[t][...]
    tile = total // 4
    at = 0
    for left in range(4):
        for right in range(left, 4):
            block = packed_ref[at * tile : (at + 1) * tile, :]
            a = slice(left * tile, (left + 1) * tile)
            b = slice(right * tile, (right + 1) * tile)
            gram_ref[a, b] = block
            if left != right:
                gram_ref[b, a] = block.T
            at += 1
    gram = gram_ref[...]
    gram_norm = jnp.sqrt(jnp.sum(gram * gram, keepdims=True) + EPSILON)
    eye = (
        lax.broadcasted_iota(jnp.int32, (total, total), 0) == lax.broadcasted_iota(jnp.int32, (total, total), 1)
    ).astype(jnp.float32)

    def mul(a, b):
        ah, al = split(a)
        bh, bl = split(b)
        return dot(ah, bh) + (dot(ah, bl) + dot(al, bh))

    approx = gram / gram_norm
    inverse = None
    for step in range(NS_ITERS):
        product = approx if inverse is None else mul(inverse, approx)
        correction = (3.0 * eye - product) * 0.5
        if step + 1 < NS_ITERS:
            approx = mul(approx, correction)
        inverse = correction if inverse is None else mul(correction, inverse)
    rotation = inverse.T * jnp.sqrt(scale_rows / gram_norm)
    hi, lo = split(rotation)
    hi_ref[...] = hi
    lo_ref[...] = lo


def inverse_of(me, pieces, total, scale_rows):
    parts = len(pieces)
    tile = total // 4
    vmem = pl.BlockSpec(memory_space=pltpu.VMEM)
    return pl.pallas_call(
        functools.partial(inverse_kernel, parts=parts, total=total, scale_rows=scale_rows),
        out_shape=[jax.ShapeDtypeStruct((total, total), jnp.bfloat16)] * 2,
        in_specs=[pl.BlockSpec(memory_space=pltpu.SMEM)] + [vmem] * parts,
        out_specs=[vmem] * 2,
        scratch_shapes=[pltpu.VMEM((10 * tile, tile), jnp.float32), pltpu.VMEM((total, total), jnp.float32)],
        compiler_params=pltpu.CompilerParams(vmem_limit_bytes=VMEM_LIMIT),
        name="inverse_of",
    )(me, *pieces)


def rotate_kernel(me_ref, rh_ref, rl_ref, hi_ref, lo_ref, *refs, parts):
    outs, stage_ref = refs[:parts], refs[parts]
    me = me_ref[0]
    vec_count = outs[0].shape[0]
    hi, lo = hi_ref[...], lo_ref[...]
    stage_ref[...] = dot(rh_ref[...], hi) + (dot(rh_ref[...], lo) + dot(rl_ref[...], hi))
    for t in range(parts):
        place = pl.multiple_of(jnp.bitwise_xor(me, t) * vec_count, vec_count)
        outs[t][...] = stage_ref[pl.ds(place, vec_count), :]


def rotate_step(me, rot_hi, rot_lo, hi, lo, parts):
    total, length = hi.shape
    vmem = pl.BlockSpec(memory_space=pltpu.VMEM)
    return pl.pallas_call(
        functools.partial(rotate_kernel, parts=parts),
        out_shape=[jax.ShapeDtypeStruct((total // parts, length), jnp.float32)] * parts,
        in_specs=[pl.BlockSpec(memory_space=pltpu.SMEM)] + [vmem] * 4,
        out_specs=[vmem] * parts,
        scratch_shapes=[pltpu.VMEM((total, length), jnp.float32)],
        compiler_params=pltpu.CompilerParams(vmem_limit_bytes=VMEM_LIMIT),
        cost_estimate=pl.CostEstimate(
            flops=6 * total * total * length, transcendentals=0, bytes_accessed=8 * total * length
        ),
        name="rotate_step",
    )(me, rot_hi, rot_lo, hi, lo)


def place_kernel(me_ref, *refs, parts, offset):
    pieces = refs[:parts]
    out_ref, held_ref, sems = refs[-3:]
    me = me_ref[0]
    length = pieces[0].shape[1]
    loads = [pltpu.make_async_copy(pieces[t], held_ref.at[t], sems.at[0, t]) for t in range(parts)]
    for load in loads:
        load.start()
    stores = []
    for t in range(parts):
        loads[t].wait()
        at = pl.multiple_of(jnp.bitwise_xor(me, t) * length + offset, LANES)
        store = pltpu.make_async_copy(held_ref.at[t], out_ref.at[:, pl.ds(at, length)], sems.at[1, t])
        store.start()
        stores.append(store)
    for store in stores:
        store.wait()


def place_step(me, pieces, before, offset, shape):
    parts = len(pieces)
    anywhere = pl.BlockSpec(memory_space=pl.ANY)
    args = list(pieces) + ([] if before is None else [before])
    return pl.pallas_call(
        functools.partial(place_kernel, parts=parts, offset=offset),
        out_shape=jax.ShapeDtypeStruct(shape, jnp.float32),
        in_specs=[pl.BlockSpec(memory_space=pltpu.SMEM)] + [anywhere] * len(args),
        out_specs=anywhere,
        scratch_shapes=[
            pltpu.VMEM((parts,) + pieces[0].shape, jnp.float32),
            pltpu.SemaphoreType.DMA((2, parts)),
        ],
        input_output_aliases={} if before is None else {1 + parts: 0},
        name="place_step",
    )(me, *args)


def exchange(pieces, axis):
    count = len(pieces)
    return [pieces[0]] + [lax.ppermute(pieces[t], axis, [(i, i ^ t) for i in range(count)]) for t in range(1, count)]


def on_device(vectors, col_blocks, op_ids, coefficients, onsite, phonon_ops):
    vec_count, row_count = vectors.shape
    op_count, block_size = phonon_ops.shape[0], phonon_ops.shape[1]
    per_row = col_blocks.shape[1]
    block_count = row_count // block_size
    parts = lax.axis_size("vec")
    row_axis = lax.axis_size("row")
    groups = 4 if parts <= 8 else 1
    group_chunks = block_count // BAND // groups
    part_blocks = block_count // groups // parts
    me = lax.axis_index("vec").astype(jnp.int32)[None]
    first_block = lax.axis_index("row") * block_count
    upward = [(i, i + 1) for i in range(row_axis - 1)]
    downward = [(i + 1, i) for i in range(row_axis - 1)]

    halo = 2 * BAND * block_size
    low_vectors = lax.ppermute(vectors[:, row_count - halo :], "row", upward)
    high_vectors = lax.ppermute(vectors[:, :halo], "row", downward)
    code = (col_blocks * op_count + op_ids).reshape(-1)
    coef = coefficients.reshape(-1)
    tail = BAND * per_row
    ends = [
        jnp.concatenate([code[a:b].astype(jnp.float32), coef[a:b], onsite[c:d]])
        for a, b, c, d in (
            (code.shape[0] - tail, code.shape[0], row_count - BAND * block_size, row_count),
            (0, tail, 0, BAND * block_size),
        )
    ]
    low_end = lax.ppermute(ends[0], "row", upward)
    high_end = lax.ppermute(ends[1], "row", downward)

    def index_of(code):
        column = code // op_count - first_block + 2 * BAND
        column = jnp.clip(column, 0, block_count + 4 * BAND - 1)
        chunk = (column // BAND) % RING
        return chunk * (BAND * op_count) + (column % BAND) * op_count + code % op_count

    idx = index_of(code)
    onsite_row = onsite[None, :]
    full_idx = index_of(
        jnp.concatenate([low_end[:tail].astype(jnp.int32), code, high_end[:tail].astype(jnp.int32)])
    )
    full_coef = jnp.concatenate([low_end[tail : 2 * tail], coef, high_end[tail : 2 * tail]])
    full_onsite = jnp.concatenate([low_end[2 * tail :], onsite, high_end[2 * tail :]])[None, :]

    w_op = jnp.transpose(phonon_ops, (2, 0, 1)).reshape(block_size, op_count * block_size)
    w_high = lax.reduce_precision(w_op, 8, 7)
    w = jnp.concatenate([w_high, w_high, w_op - w_high], axis=0).astype(jnp.bfloat16)

    def first(start, count, low=None, high=None):
        edge = low is not None or high is not None
        return apply_ham(
            me,
            full_idx if edge else idx,
            full_coef if edge else coef,
            full_onsite if edge else onsite_row,
            w,
            vectors,
            max(start - 2, 0),
            count,
            start if edge else start - 1,
            start,
            start if edge else start - 1,
            low=low,
            high=high,
            op_count=op_count,
            per_row=per_row,
        )[0]

    def second(group, main, main_chunk, **kwargs):
        start = group * group_chunks
        return apply_ham(
            me, idx, coef, onsite_row, w, main, main_chunk, group_chunks, start, start + 1, start,
            base=vectors, base_chunk=start, parts=parts, part_blocks=part_blocks, op_count=op_count, per_row=per_row, **kwargs,
        )

    n = group_chunks
    received = {}
    if groups == 1:
        steps = first(0, n + 2, low=low_vectors, high=high_vectors)
        received[0] = exchange(second(0, steps, 0), "vec")
        order = [0]
    else:
        order = [1, 2, 3, 0]
        step_1 = first(n, n + 2)
        received[1] = exchange(second(1, step_1, 0), "vec")
        step_2 = first(2 * n + 2, n)
        received[2] = exchange(second(2, step_2, 0, low=step_1, low_chunk=n), "vec")
        step_3 = first(3 * n + 2, n, high=high_vectors)
        received[3] = exchange(second(3, step_3, 0, low=step_2, low_chunk=n - 2), "vec")
        step_0 = first(0, n, low=low_vectors)
        received[0] = exchange(second(0, step_0, 0, high=step_1, high_chunk=0), "vec")

    stacks = {}
    partial_gram = None
    for place, group in enumerate(order):
        last = place + 1 == len(order)
        out = gram_step(me, received[group], partial_gram, last)
        stacks[group] = (out[0], out[1])
        partial_gram = out[2]
    mine = sum_of(exchange(out[2:], "vec"))
    summed = sum_of(
        [mine] + [lax.ppermute(mine, "row", [(i, i ^ k) for i in range(row_axis)]) for k in range(1, row_axis)]
    )
    shares = [summed] + [
        lax.ppermute(summed, "vec", [(i, i ^ t) for i in range(parts)]) for t in range(1, parts)
    ]
    rot_hi, rot_lo = inverse_of(me, shares, vec_count * parts, float(row_count * row_axis))

    result = None
    for group in order:
        pieces = exchange(rotate_step(me, rot_hi, rot_lo, *stacks[group], parts), "vec")
        result = place_step(me, pieces, result, group * (row_count // groups), vectors.shape)
    return result


def solution(mesh):
    return jax.shard_map(
        on_device,
        mesh=mesh,
        in_specs=(P("vec", "row"), P("row", None), P("row", None), P("row", None), P("row"), P()),
        out_specs=P("vec", "row"),
        check_vma=False,
    )
```

```python
import functools

import jax
import jax.numpy as jnp
from jax import lax
from jax.experimental import pallas as pl
from jax.experimental.pallas import tpu as pltpu
from jax.sharding import PartitionSpec as P

BAND = 8
NS_ITERS = 3
CENTER = 0.25
HALF_WIDTH = 2.0
EPSILON = 1e-06
LANES = 128
RING = 3
VMEM_LIMIT = 58 * 1024 * 1024


def split(x):
    hi = x.astype(jnp.bfloat16)
    lo = (x - hi.astype(jnp.float32)).astype(jnp.bfloat16)
    return hi, lo


def dot(a, b):
    return jnp.dot(a, b, preferred_element_type=jnp.float32)


def ham_kernel(
    me_ref, idx_ref, coef_ref, *refs, steps, row_base, ring_base, op_count, per_row, has_low, has_high, second, parts, part_blocks
):
    refs = list(refs)
    main_ref = refs.pop(0)
    low_ref = refs.pop(0) if has_low else None
    high_ref = refs.pop(0) if has_high else None
    onsite_ref = refs.pop(0)
    base_ref = refs.pop(0) if second else None
    w_ref = refs.pop(0)
    outs = [refs.pop(0) for _ in range(parts if second else 1)]
    ring_ref = refs.pop(0)
    self_ref = refs.pop(0)
    stage_ref = refs.pop(0) if second else None
    i = pl.program_id(0)
    vec_count = main_ref.shape[0]
    source = main_ref[...]
    if has_low:
        source = jnp.where(i < 2, low_ref[...], source)
    if has_high:
        source = jnp.where(i >= steps - 2, high_ref[...], source)
    slot = lax.rem(i + ring_base, RING) * (BAND * op_count)
    x = jnp.concatenate([source[:, g * LANES : (g + 1) * LANES] for g in range(BAND)], axis=0)
    hi, lo = split(x)
    lhs = jnp.concatenate([hi, lo, hi], axis=1)
    for o in range(0, op_count, 2):
        t = dot(lhs, w_ref[:, o * LANES : (o + 2) * LANES])
        for g in range(BAND):
            for k in range(2):
                ring_ref[slot + g * op_count + o + k] = t[
                    g * vec_count : (g + 1) * vec_count, k * LANES : (k + 1) * LANES
                ]

    @pl.when(i >= 2)
    def _():
        previous = lax.rem(i + 1, 2)
        for g in range(BAND):
            block = (i - 2) * BAND + g
            row = (block + row_base) * per_row
            span = slice(g * LANES, (g + 1) * LANES)
            own = self_ref[previous, :, span]
            acc = (onsite_ref[:, span] - CENTER) * own
            for j in range(per_row):
                acc = acc + coef_ref[row + j] * ring_ref[idx_ref[row + j]]
            if second:
                acc = acc - base_ref[:, span]
                peer = lax.div(block, part_blocks)
                place = jnp.bitwise_xor(peer, me_ref[0]) * part_blocks + lax.rem(block, part_blocks)
                stage_ref[place] = acc
            else:
                outs[0][:, span] = acc * (1.0 / HALF_WIDTH)

    self_ref[lax.rem(i, 2)] = source
    if second:

        @pl.when(i == steps - 1)
        def _():
            for part in range(parts):
                for s in range(part_blocks):
                    outs[part][:, s * LANES : (s + 1) * LANES] = stage_ref[part * part_blocks + s]


def apply_ham(
    me, idx, coef, onsite, w, main, main_chunk, chunks, row_chunk, ring_base, onsite_chunk,
    low=None, low_chunk=0, high=None, high_chunk=0, base=None, base_chunk=0, parts=0, part_blocks=1, op_count=16, per_row=16,
):
    vec_count = main.shape[0]
    width = BAND * LANES
    steps = chunks + 2
    second = base is not None
    main_first = 2 if low is not None else 0
    main_last = steps - 1 - (2 if high is not None else 0)
    spec = functools.partial(pl.BlockSpec, (vec_count, width))
    in_specs = [spec(lambda i, *_: (0, jnp.clip(i, main_first, main_last) - main_first + main_chunk))]
    args = [main]
    if low is not None:
        in_specs.append(spec(lambda i, *_: (0, jnp.clip(i, 0, 1) + low_chunk)))
        args.append(low)
    if high is not None:
        in_specs.append(spec(lambda i, *_: (0, jnp.clip(i - (steps - 2), 0, 1) + high_chunk)))
        args.append(high)
    in_specs.append(pl.BlockSpec((1, width), lambda i, *_: (0, jnp.maximum(i - 2, 0) + onsite_chunk)))
    args.append(onsite)
    if second:
        in_specs.append(spec(lambda i, *_: (0, jnp.maximum(i - 2, 0) + base_chunk)))
        args.append(base)
    in_specs.append(pl.BlockSpec(w.shape, lambda i, *_: (0, 0)))
    args.append(w)
    scratch = [
        pltpu.VMEM((RING * BAND * op_count, vec_count, LANES), jnp.float32),
        pltpu.VMEM((2, vec_count, width), jnp.float32),
    ]
    if second:
        out_shape = [jax.ShapeDtypeStruct((vec_count, part_blocks * LANES), jnp.float32)] * parts
        out_specs = [pl.BlockSpec((vec_count, part_blocks * LANES), lambda i, *_: (0, 0))] * parts
        scratch.append(pltpu.VMEM((parts * part_blocks, vec_count, LANES), jnp.float32))
    else:
        out_shape = [jax.ShapeDtypeStruct((vec_count, chunks * width), jnp.float32)]
        out_specs = [spec(lambda i, *_: (0, jnp.maximum(i - 2, 0)))]
    flops = 2 * steps * BAND * vec_count * 3 * LANES * LANES * op_count
    return pl.pallas_call(
        functools.partial(
            ham_kernel,
            steps=steps,
            row_base=row_chunk * BAND,
            ring_base=ring_base,
            op_count=op_count,
            per_row=per_row,
            has_low=low is not None,
            has_high=high is not None,
            second=second,
            parts=parts,
            part_blocks=part_blocks,
        ),
        out_shape=out_shape,
        grid_spec=pltpu.PrefetchScalarGridSpec(
            num_scalar_prefetch=3, grid=(steps,), in_specs=in_specs, out_specs=out_specs, scratch_shapes=scratch
        ),
        compiler_params=pltpu.CompilerParams(vmem_limit_bytes=VMEM_LIMIT),
        cost_estimate=pl.CostEstimate(flops=2 * flops, transcendentals=0, bytes_accessed=8 * steps * vec_count * width),
        name="ham_second" if second else "ham_first",
    )(me, idx, coef, *args)


def gram_kernel(me_ref, *refs, parts, first, last):
    refs = list(refs)
    pieces = [refs.pop(0) for _ in range(parts)]
    before_ref = None if first else refs.pop(0)
    hi_ref, lo_ref = refs.pop(0), refs.pop(0)
    outs = [refs.pop(0) for _ in range(parts if last else 1)]
    stage_ref = refs.pop(0)
    me = me_ref[0]
    vec_count = pieces[0].shape[0]
    total = parts * vec_count
    for t in range(parts):
        place = pl.multiple_of(jnp.bitwise_xor(me, t) * vec_count, vec_count)
        hi, lo = split(pieces[t][...])
        hi_ref[pl.ds(place, vec_count), :] = hi
        lo_ref[pl.ds(place, vec_count), :] = lo
    contract = (((1,), (1,)), ((), ()))
    hi, lo = hi_ref[...], lo_ref[...]
    square = lax.dot_general(hi, hi, contract, preferred_element_type=jnp.float32)
    cross = lax.dot_general(hi, lo, contract, preferred_element_type=jnp.float32)
    if first:
        stage_ref[0] = square
        stage_ref[1] = cross
    else:
        stage_ref[0] = before_ref[0] + square
        stage_ref[1] = before_ref[1] + cross
    if not last:
        outs[0][...] = stage_ref[...]
    else:
        packed_ref = refs.pop(0)
        tile = total // 4
        at = 0
        for left in range(4):
            for right in range(left, 4):
                a = slice(left * tile, (left + 1) * tile)
                b = slice(right * tile, (right + 1) * tile)
                packed_ref[at * tile : (at + 1) * tile, :] = (
                    stage_ref[0, a, b] + stage_ref[1, a, b] + stage_ref[1, b, a].T
                )
                at += 1
        rows = at * tile // parts
        for t in range(parts):
            place = pl.multiple_of(jnp.bitwise_xor(me, t) * rows, 8)
            outs[t][...] = packed_ref[pl.ds(place, rows), :]


def gram_step(me, pieces, before, last):
    parts = len(pieces)
    vec_count, length = pieces[0].shape
    total = parts * vec_count
    whole = jax.ShapeDtypeStruct((total, length), jnp.bfloat16)
    tile = total // 4
    if last:
        outs = [jax.ShapeDtypeStruct((10 * tile // parts, tile), jnp.float32)] * parts
        extra = [pltpu.VMEM((10 * tile, tile), jnp.float32)]
    else:
        outs = [jax.ShapeDtypeStruct((2, total, total), jnp.float32)]
        extra = []
    vmem = pl.BlockSpec(memory_space=pltpu.VMEM)
    args = list(pieces) + ([] if before is None else [before])
    return pl.pallas_call(
        functools.partial(gram_kernel, parts=parts, first=before is None, last=last),
        out_shape=[whole, whole] + outs,
        in_specs=[pl.BlockSpec(memory_space=pltpu.SMEM)] + [vmem] * len(args),
        out_specs=[vmem] * (2 + len(outs)),
        scratch_shapes=[pltpu.VMEM((2, total, total), jnp.float32)] + extra,
        compiler_params=pltpu.CompilerParams(vmem_limit_bytes=VMEM_LIMIT),
        cost_estimate=pl.CostEstimate(
            flops=4 * total * total * length, transcendentals=0, bytes_accessed=8 * total * length
        ),
        name="gram_step",
    )(me, *args)


def sum_kernel(*refs):
    acc = refs[0][...]
    for ref in refs[1:-1]:
        acc = acc + ref[...]
    refs[-1][...] = acc


def sum_of(arrays):
    return pl.pallas_call(
        sum_kernel, out_shape=jax.ShapeDtypeStruct(arrays[0].shape, jnp.float32), name="sum_of"
    )(*arrays)


def inverse_kernel(me_ref, *refs, parts, total, scale_rows):
    pieces = refs[:parts]
    hi_ref, lo_ref, packed_ref, gram_ref = refs[parts:]
    me = me_ref[0]
    rows = pieces[0].shape[0]
    for t in range(parts):
        place = pl.multiple_of(jnp.bitwise_xor(me, t) * rows, 8)
        packed_ref[pl.ds(place, rows), :] = pieces[t][...]
    tile = total // 4
    at = 0
    for left in range(4):
        for right in range(left, 4):
            block = packed_ref[at * tile : (at + 1) * tile, :]
            a = slice(left * tile, (left + 1) * tile)
            b = slice(right * tile, (right + 1) * tile)
            gram_ref[a, b] = block
            if left != right:
                gram_ref[b, a] = block.T
            at += 1
    gram = gram_ref[...]
    gram_norm = jnp.sqrt(jnp.sum(gram * gram, keepdims=True) + EPSILON)
    eye = (
        lax.broadcasted_iota(jnp.int32, (total, total), 0) == lax.broadcasted_iota(jnp.int32, (total, total), 1)
    ).astype(jnp.float32)

    def mul(a, b):
        ah, al = split(a)
        bh, bl = split(b)
        return dot(ah, bh) + (dot(ah, bl) + dot(al, bh))

    approx = gram / gram_norm
    inverse = None
    for step in range(NS_ITERS):
        product = approx if inverse is None else mul(inverse, approx)
        correction = (3.0 * eye - product) * 0.5
        if step + 1 < NS_ITERS:
            approx = mul(approx, correction)
        inverse = correction if inverse is None else mul(correction, inverse)
    rotation = inverse.T * jnp.sqrt(scale_rows / gram_norm)
    hi, lo = split(rotation)
    hi_ref[...] = hi
    lo_ref[...] = lo


def inverse_of(me, pieces, total, scale_rows):
    parts = len(pieces)
    tile = total // 4
    vmem = pl.BlockSpec(memory_space=pltpu.VMEM)
    return pl.pallas_call(
        functools.partial(inverse_kernel, parts=parts, total=total, scale_rows=scale_rows),
        out_shape=[jax.ShapeDtypeStruct((total, total), jnp.bfloat16)] * 2,
        in_specs=[pl.BlockSpec(memory_space=pltpu.SMEM)] + [vmem] * parts,
        out_specs=[vmem] * 2,
        scratch_shapes=[pltpu.VMEM((10 * tile, tile), jnp.float32), pltpu.VMEM((total, total), jnp.float32)],
        compiler_params=pltpu.CompilerParams(vmem_limit_bytes=VMEM_LIMIT),
        name="inverse_of",
    )(me, *pieces)


def rotate_kernel(me_ref, rh_ref, rl_ref, hi_ref, lo_ref, *refs, parts):
    outs, stage_ref = refs[:parts], refs[parts]
    me = me_ref[0]
    vec_count = outs[0].shape[0]
    hi, lo = hi_ref[...], lo_ref[...]
    stage_ref[...] = dot(rh_ref[...], hi) + (dot(rh_ref[...], lo) + dot(rl_ref[...], hi))
    for t in range(parts):
        place = pl.multiple_of(jnp.bitwise_xor(me, t) * vec_count, vec_count)
        outs[t][...] = stage_ref[pl.ds(place, vec_count), :]


def rotate_step(me, rot_hi, rot_lo, hi, lo, parts):
    total, length = hi.shape
    vmem = pl.BlockSpec(memory_space=pltpu.VMEM)
    return pl.pallas_call(
        functools.partial(rotate_kernel, parts=parts),
        out_shape=[jax.ShapeDtypeStruct((total // parts, length), jnp.float32)] * parts,
        in_specs=[pl.BlockSpec(memory_space=pltpu.SMEM)] + [vmem] * 4,
        out_specs=[vmem] * parts,
        scratch_shapes=[pltpu.VMEM((total, length), jnp.float32)],
        compiler_params=pltpu.CompilerParams(vmem_limit_bytes=VMEM_LIMIT),
        cost_estimate=pl.CostEstimate(
            flops=6 * total * total * length, transcendentals=0, bytes_accessed=8 * total * length
        ),
        name="rotate_step",
    )(me, rot_hi, rot_lo, hi, lo)


def place_kernel(me_ref, *refs, parts, offset):
    pieces = refs[:parts]
    out_ref, held_ref, sems = refs[-3:]
    me = me_ref[0]
    length = pieces[0].shape[1]
    loads = [pltpu.make_async_copy(pieces[t], held_ref.at[t], sems.at[0, t]) for t in range(parts)]
    for load in loads:
        load.start()
    stores = []
    for t in range(parts):
        loads[t].wait()
        at = pl.multiple_of(jnp.bitwise_xor(me, t) * length + offset, LANES)
        store = pltpu.make_async_copy(held_ref.at[t], out_ref.at[:, pl.ds(at, length)], sems.at[1, t])
        store.start()
        stores.append(store)
    for store in stores:
        store.wait()


def place_step(me, pieces, before, offset, shape):
    parts = len(pieces)
    anywhere = pl.BlockSpec(memory_space=pl.ANY)
    args = list(pieces) + ([] if before is None else [before])
    return pl.pallas_call(
        functools.partial(place_kernel, parts=parts, offset=offset),
        out_shape=jax.ShapeDtypeStruct(shape, jnp.float32),
        in_specs=[pl.BlockSpec(memory_space=pltpu.SMEM)] + [anywhere] * len(args),
        out_specs=anywhere,
        scratch_shapes=[
            pltpu.VMEM((parts,) + pieces[0].shape, jnp.float32),
            pltpu.SemaphoreType.DMA((2, parts)),
        ],
        input_output_aliases={} if before is None else {1 + parts: 0},
        name="place_step",
    )(me, *args)


def exchange(pieces, axis):
    count = len(pieces)
    return [pieces[0]] + [lax.ppermute(pieces[t], axis, [(i, i ^ t) for i in range(count)]) for t in range(1, count)]


def on_device(vectors, col_blocks, op_ids, coefficients, onsite, phonon_ops):
    vec_count, row_count = vectors.shape
    op_count, block_size = phonon_ops.shape[0], phonon_ops.shape[1]
    per_row = col_blocks.shape[1]
    block_count = row_count // block_size
    parts = lax.axis_size("vec")
    row_axis = lax.axis_size("row")
    bands = block_count // BAND
    if parts <= 8 and bands % 4 == 0 and (bands // 4 * BAND) % parts == 0:
        middle, high_group, low_group = (bands // 4, bands // 2), (3 * bands // 4, bands // 4), (0, bands // 4)
        order = [middle, high_group, low_group]
    else:
        order = [(0, bands)]
    me = lax.axis_index("vec").astype(jnp.int32)[None]
    first_block = lax.axis_index("row") * block_count
    upward = [(i, i + 1) for i in range(row_axis - 1)]
    downward = [(i + 1, i) for i in range(row_axis - 1)]

    def index_of(code):
        column = jnp.maximum(code // op_count - first_block + 2 * BAND, 0)
        return column % (RING * BAND) * op_count + code % op_count

    def with_ends(low_part, middle, high_part):
        return jnp.concatenate([low_part, middle, high_part])

    code = (col_blocks * op_count + op_ids).reshape(-1)
    coef = coefficients.reshape(-1)
    tail = BAND * per_row
    no_rows = jnp.zeros((tail,), jnp.int32)
    no_site = jnp.zeros((BAND * block_size,), jnp.float32)
    inner = (
        index_of(with_ends(no_rows, code, no_rows)),
        with_ends(no_site[:tail], coef, no_site[:tail]),
        with_ends(no_site, onsite, no_site)[None, :],
    )

    w_op = jnp.transpose(phonon_ops, (2, 0, 1)).reshape(block_size, op_count * block_size)
    w_high = lax.reduce_precision(w_op, 8, 7)
    w = jnp.concatenate([w_high, w_high, w_op - w_high], axis=0).astype(jnp.bfloat16)

    def first(table, start, count, low=None, high=None):
        return apply_ham(
            me, *table, w, vectors, max(start - 2, 0), count, start, start, start,
            low=low, high=high, op_count=op_count, per_row=per_row,
        )[0]

    def second(group, main, main_chunk, **kwargs):
        start, count = group
        part_blocks = count * BAND // parts
        return apply_ham(
            me, *inner, w, main, main_chunk, count, start + 1, start + 1, start + 1,
            base=vectors, base_chunk=start, parts=parts, part_blocks=part_blocks, op_count=op_count, per_row=per_row, **kwargs,
        )

    received = {}
    halo = 2 * BAND * block_size
    ends = [
        jnp.concatenate([code[a:b].astype(jnp.float32), coef[a:b], onsite[c:d]])
        for a, b, c, d in (
            (code.shape[0] - tail, code.shape[0], row_count - BAND * block_size, row_count),
            (0, tail, 0, BAND * block_size),
        )
    ]
    edges = [vectors[:, row_count - halo :], vectors[:, :halo]]
    if len(order) > 1:
        step_mid = first(inner, middle[0], middle[1] + 2)
        step_mid, ends, edges = lax.optimization_barrier((step_mid, ends, edges))
    low_vectors = lax.ppermute(edges[0], "row", upward)
    high_vectors = lax.ppermute(edges[1], "row", downward)
    low_end = lax.ppermute(ends[0], "row", upward)
    high_end = lax.ppermute(ends[1], "row", downward)
    outer = (
        index_of(with_ends(low_end[:tail].astype(jnp.int32), code, high_end[:tail].astype(jnp.int32))),
        with_ends(low_end[tail : 2 * tail], coef, high_end[tail : 2 * tail]),
        with_ends(low_end[2 * tail :], onsite, high_end[2 * tail :])[None, :],
    )
    if len(order) == 1:
        steps = first(outer, 0, bands + 2, low=low_vectors, high=high_vectors)
        received[order[0]] = exchange(second(order[0], steps, 0), "vec")
    else:
        received[middle] = exchange(second(middle, step_mid, 0), "vec")
        step_high = first(outer, high_group[0] + 2, high_group[1], high=high_vectors)
        received[high_group] = exchange(
            second(high_group, step_high, 0, low=step_mid, low_chunk=middle[1]), "vec"
        )
        step_low = first(outer, 0, low_group[1], low=low_vectors)
        received[low_group] = exchange(second(low_group, step_low, 0, high=step_mid, high_chunk=0), "vec")

    stacks = {}
    partial_gram = None
    for place, group in enumerate(order):
        last = place + 1 == len(order)
        out = gram_step(me, received[group], partial_gram, last)
        stacks[group] = (out[0], out[1])
        partial_gram = out[2]
    mine = sum_of(exchange(out[2:], "vec"))
    summed = sum_of(
        [mine] + [lax.ppermute(mine, "row", [(i, i ^ k) for i in range(row_axis)]) for k in range(1, row_axis)]
    )
    shares = [summed] + [
        lax.ppermute(summed, "vec", [(i, i ^ t) for i in range(parts)]) for t in range(1, parts)
    ]
    rot_hi, rot_lo = inverse_of(me, shares, vec_count * parts, float(row_count * row_axis))

    result = None
    for group in order[1:2] + order[:1] + order[2:]:
        pieces = exchange(rotate_step(me, rot_hi, rot_lo, *stacks[group], parts), "vec")
        result = place_step(me, pieces, result, group[0] * BAND * block_size, vectors.shape)
    return result


def solution(mesh):
    return jax.shard_map(
        on_device,
        mesh=mesh,
        in_specs=(P("vec", "row"), P("row", None), P("row", None), P("row", None), P("row"), P()),
        out_specs=P("vec", "row"),
        check_vma=False,
    )
```

```python
import functools

import jax
import jax.numpy as jnp
from jax import lax
from jax.experimental import pallas as pl
from jax.experimental.pallas import tpu as pltpu
from jax.sharding import PartitionSpec as P

BAND = 8
NS_ITERS = 3
CENTER = 0.25
HALF_WIDTH = 2.0
EPSILON = 1e-06
LANES = 128
RING = 3
VMEM_LIMIT = 58 * 1024 * 1024


def split(x):
    hi = x.astype(jnp.bfloat16)
    lo = (x - hi.astype(jnp.float32)).astype(jnp.bfloat16)
    return hi, lo


def dot(a, b):
    return jnp.dot(a, b, preferred_element_type=jnp.float32)


def ham_kernel(
    me_ref, idx_ref, coef_ref, *refs, steps, row_base, ring_base, op_count, per_row, has_low, has_high, second, parts, part_blocks
):
    refs = list(refs)
    main_ref = refs.pop(0)
    low_ref = refs.pop(0) if has_low else None
    high_ref = refs.pop(0) if has_high else None
    onsite_ref = refs.pop(0)
    base_ref = refs.pop(0) if second else None
    w_ref = refs.pop(0)
    outs = [refs.pop(0) for _ in range(parts if second else 1)]
    ring_ref = refs.pop(0)
    self_ref = refs.pop(0)
    stage_ref = refs.pop(0) if second else None
    i = pl.program_id(0)
    vec_count = main_ref.shape[0]
    source = main_ref[...]
    if has_low:
        source = jnp.where(i < 2, low_ref[...], source)
    if has_high:
        source = jnp.where(i >= steps - 2, high_ref[...], source)
    slot = lax.rem(i + ring_base, RING) * (BAND * op_count)
    x = jnp.concatenate([source[:, g * LANES : (g + 1) * LANES] for g in range(BAND)], axis=0)
    hi, lo = split(x)
    lhs = jnp.concatenate([hi, lo, hi], axis=1)
    for o in range(0, op_count, 2):
        t = dot(lhs, w_ref[:, o * LANES : (o + 2) * LANES])
        for g in range(BAND):
            for k in range(2):
                ring_ref[slot + g * op_count + o + k] = t[
                    g * vec_count : (g + 1) * vec_count, k * LANES : (k + 1) * LANES
                ]

    @pl.when(i >= 2)
    def _():
        previous = lax.rem(i + 1, 2)
        for g in range(BAND):
            block = (i - 2) * BAND + g
            row = (block + row_base) * per_row
            span = slice(g * LANES, (g + 1) * LANES)
            own = self_ref[previous, :, span]
            acc = (onsite_ref[:, span] - CENTER) * own
            for j in range(per_row):
                acc = acc + coef_ref[row + j] * ring_ref[idx_ref[row + j]]
            if second:
                acc = acc - base_ref[:, span]
                peer = lax.div(block, part_blocks)
                place = jnp.bitwise_xor(peer, me_ref[0]) * part_blocks + lax.rem(block, part_blocks)
                stage_ref[place] = acc
            else:
                outs[0][:, span] = acc * (1.0 / HALF_WIDTH)

    self_ref[lax.rem(i, 2)] = source
    if second:

        @pl.when(i == steps - 1)
        def _():
            for part in range(parts):
                for s in range(part_blocks):
                    outs[part][:, s * LANES : (s + 1) * LANES] = stage_ref[part * part_blocks + s]


def apply_ham(
    me, idx, coef, onsite, w, main, main_chunk, chunks, row_chunk, ring_base, onsite_chunk,
    low=None, low_chunk=0, high=None, high_chunk=0, base=None, base_chunk=0, parts=0, part_blocks=1, op_count=16, per_row=16,
):
    vec_count = main.shape[0]
    width = BAND * LANES
    steps = chunks + 2
    second = base is not None
    main_first = 2 if low is not None else 0
    main_last = steps - 1 - (2 if high is not None else 0)
    spec = functools.partial(pl.BlockSpec, (vec_count, width))
    in_specs = [spec(lambda i, *_: (0, jnp.clip(i, main_first, main_last) - main_first + main_chunk))]
    args = [main]
    if low is not None:
        in_specs.append(spec(lambda i, *_: (0, jnp.clip(i, 0, 1) + low_chunk)))
        args.append(low)
    if high is not None:
        in_specs.append(spec(lambda i, *_: (0, jnp.clip(i - (steps - 2), 0, 1) + high_chunk)))
        args.append(high)
    in_specs.append(pl.BlockSpec((1, width), lambda i, *_: (0, jnp.maximum(i - 2, 0) + onsite_chunk)))
    args.append(onsite)
    if second:
        in_specs.append(spec(lambda i, *_: (0, jnp.maximum(i - 2, 0) + base_chunk)))
        args.append(base)
    in_specs.append(pl.BlockSpec(w.shape, lambda i, *_: (0, 0)))
    args.append(w)
    scratch = [
        pltpu.VMEM((RING * BAND * op_count, vec_count, LANES), jnp.float32),
        pltpu.VMEM((2, vec_count, width), jnp.float32),
    ]
    if second:
        out_shape = [jax.ShapeDtypeStruct((vec_count, part_blocks * LANES), jnp.float32)] * parts
        out_specs = [pl.BlockSpec((vec_count, part_blocks * LANES), lambda i, *_: (0, 0))] * parts
        scratch.append(pltpu.VMEM((parts * part_blocks, vec_count, LANES), jnp.float32))
    else:
        out_shape = [jax.ShapeDtypeStruct((vec_count, chunks * width), jnp.float32)]
        out_specs = [spec(lambda i, *_: (0, jnp.maximum(i - 2, 0)))]
    flops = 2 * steps * BAND * vec_count * 3 * LANES * LANES * op_count
    return pl.pallas_call(
        functools.partial(
            ham_kernel,
            steps=steps,
            row_base=row_chunk * BAND,
            ring_base=ring_base,
            op_count=op_count,
            per_row=per_row,
            has_low=low is not None,
            has_high=high is not None,
            second=second,
            parts=parts,
            part_blocks=part_blocks,
        ),
        out_shape=out_shape,
        grid_spec=pltpu.PrefetchScalarGridSpec(
            num_scalar_prefetch=3, grid=(steps,), in_specs=in_specs, out_specs=out_specs, scratch_shapes=scratch
        ),
        compiler_params=pltpu.CompilerParams(vmem_limit_bytes=VMEM_LIMIT),
        cost_estimate=pl.CostEstimate(flops=2 * flops, transcendentals=0, bytes_accessed=8 * steps * vec_count * width),
        name="ham_second" if second else "ham_first",
    )(me, idx, coef, *args)


def gram_kernel(me_ref, *refs, parts, first, last):
    refs = list(refs)
    pieces = [refs.pop(0) for _ in range(parts)]
    before_ref = None if first else refs.pop(0)
    hi_ref, lo_ref = refs.pop(0), refs.pop(0)
    outs = [refs.pop(0) for _ in range(parts if last else 1)]
    stage_ref = refs.pop(0)
    me = me_ref[0]
    vec_count = pieces[0].shape[0]
    total = parts * vec_count
    for t in range(parts):
        place = pl.multiple_of(jnp.bitwise_xor(me, t) * vec_count, vec_count)
        hi, lo = split(pieces[t][...])
        hi_ref[pl.ds(place, vec_count), :] = hi
        lo_ref[pl.ds(place, vec_count), :] = lo
    contract = (((1,), (1,)), ((), ()))
    hi, lo = hi_ref[...], lo_ref[...]
    square = lax.dot_general(hi, hi, contract, preferred_element_type=jnp.float32)
    cross = lax.dot_general(hi, lo, contract, preferred_element_type=jnp.float32)
    if first:
        stage_ref[0] = square
        stage_ref[1] = cross
    else:
        stage_ref[0] = before_ref[0] + square
        stage_ref[1] = before_ref[1] + cross
    if not last:
        outs[0][...] = stage_ref[...]
    else:
        packed_ref = refs.pop(0)
        tile = total // 4
        at = 0
        for left in range(4):
            for right in range(left, 4):
                a = slice(left * tile, (left + 1) * tile)
                b = slice(right * tile, (right + 1) * tile)
                packed_ref[at * tile : (at + 1) * tile, :] = (
                    stage_ref[0, a, b] + stage_ref[1, a, b] + stage_ref[1, b, a].T
                )
                at += 1
        rows = at * tile // parts
        for t in range(parts):
            place = pl.multiple_of(jnp.bitwise_xor(me, t) * rows, 8)
            outs[t][...] = packed_ref[pl.ds(place, rows), :]


def gram_step(me, pieces, before, last):
    parts = len(pieces)
    vec_count, length = pieces[0].shape
    total = parts * vec_count
    whole = jax.ShapeDtypeStruct((total, length), jnp.bfloat16)
    tile = total // 4
    if last:
        outs = [jax.ShapeDtypeStruct((10 * tile // parts, tile), jnp.float32)] * parts
        extra = [pltpu.VMEM((10 * tile, tile), jnp.float32)]
    else:
        outs = [jax.ShapeDtypeStruct((2, total, total), jnp.float32)]
        extra = []
    vmem = pl.BlockSpec(memory_space=pltpu.VMEM)
    args = list(pieces) + ([] if before is None else [before])
    return pl.pallas_call(
        functools.partial(gram_kernel, parts=parts, first=before is None, last=last),
        out_shape=[whole, whole] + outs,
        in_specs=[pl.BlockSpec(memory_space=pltpu.SMEM)] + [vmem] * len(args),
        out_specs=[vmem] * (2 + len(outs)),
        scratch_shapes=[pltpu.VMEM((2, total, total), jnp.float32)] + extra,
        compiler_params=pltpu.CompilerParams(vmem_limit_bytes=VMEM_LIMIT),
        cost_estimate=pl.CostEstimate(
            flops=4 * total * total * length, transcendentals=0, bytes_accessed=8 * total * length
        ),
        name="gram_step",
    )(me, *args)


def sum_kernel(*refs):
    acc = refs[0][...]
    for ref in refs[1:-1]:
        acc = acc + ref[...]
    refs[-1][...] = acc


def sum_of(arrays):
    return pl.pallas_call(
        sum_kernel, out_shape=jax.ShapeDtypeStruct(arrays[0].shape, jnp.float32), name="sum_of"
    )(*arrays)


def inverse_kernel(me_ref, *refs, parts, total, scale_rows):
    pieces = refs[:parts]
    hi_ref, lo_ref, packed_ref, gram_ref = refs[parts:]
    me = me_ref[0]
    rows = pieces[0].shape[0]
    for t in range(parts):
        place = pl.multiple_of(jnp.bitwise_xor(me, t) * rows, 8)
        packed_ref[pl.ds(place, rows), :] = pieces[t][...]
    tile = total // 4
    at = 0
    for left in range(4):
        for right in range(left, 4):
            block = packed_ref[at * tile : (at + 1) * tile, :]
            a = slice(left * tile, (left + 1) * tile)
            b = slice(right * tile, (right + 1) * tile)
            gram_ref[a, b] = block
            if left != right:
                gram_ref[b, a] = block.T
            at += 1
    gram = gram_ref[...]
    gram_norm = jnp.sqrt(jnp.sum(gram * gram, keepdims=True) + EPSILON)
    eye = (
        lax.broadcasted_iota(jnp.int32, (total, total), 0) == lax.broadcasted_iota(jnp.int32, (total, total), 1)
    ).astype(jnp.float32)

    def mul(a, b):
        ah, al = split(a)
        bh, bl = split(b)
        return dot(ah, bh) + (dot(ah, bl) + dot(al, bh))

    approx = gram / gram_norm
    inverse = None
    for step in range(NS_ITERS):
        product = approx if inverse is None else mul(inverse, approx)
        correction = (3.0 * eye - product) * 0.5
        if step + 1 < NS_ITERS:
            approx = mul(approx, correction)
        inverse = correction if inverse is None else mul(correction, inverse)
    rotation = inverse.T * jnp.sqrt(scale_rows / gram_norm)
    hi, lo = split(rotation)
    hi_ref[...] = hi
    lo_ref[...] = lo


def inverse_of(me, pieces, total, scale_rows):
    parts = len(pieces)
    tile = total // 4
    vmem = pl.BlockSpec(memory_space=pltpu.VMEM)
    return pl.pallas_call(
        functools.partial(inverse_kernel, parts=parts, total=total, scale_rows=scale_rows),
        out_shape=[jax.ShapeDtypeStruct((total, total), jnp.bfloat16)] * 2,
        in_specs=[pl.BlockSpec(memory_space=pltpu.SMEM)] + [vmem] * parts,
        out_specs=[vmem] * 2,
        scratch_shapes=[pltpu.VMEM((10 * tile, tile), jnp.float32), pltpu.VMEM((total, total), jnp.float32)],
        compiler_params=pltpu.CompilerParams(vmem_limit_bytes=VMEM_LIMIT),
        name="inverse_of",
    )(me, *pieces)


def rotate_kernel(me_ref, rh_ref, rl_ref, hi_ref, lo_ref, *refs, parts):
    outs, stage_ref = refs[:parts], refs[parts]
    me = me_ref[0]
    vec_count = outs[0].shape[0]
    hi, lo = hi_ref[...], lo_ref[...]
    stage_ref[...] = dot(rh_ref[...], hi) + (dot(rh_ref[...], lo) + dot(rl_ref[...], hi))
    for t in range(parts):
        place = pl.multiple_of(jnp.bitwise_xor(me, t) * vec_count, vec_count)
        outs[t][...] = stage_ref[pl.ds(place, vec_count), :]


def rotate_step(me, rot_hi, rot_lo, hi, lo, parts):
    total, length = hi.shape
    vmem = pl.BlockSpec(memory_space=pltpu.VMEM)
    return pl.pallas_call(
        functools.partial(rotate_kernel, parts=parts),
        out_shape=[jax.ShapeDtypeStruct((total // parts, length), jnp.float32)] * parts,
        in_specs=[pl.BlockSpec(memory_space=pltpu.SMEM)] + [vmem] * 4,
        out_specs=[vmem] * parts,
        scratch_shapes=[pltpu.VMEM((total, length), jnp.float32)],
        compiler_params=pltpu.CompilerParams(vmem_limit_bytes=VMEM_LIMIT),
        cost_estimate=pl.CostEstimate(
            flops=6 * total * total * length, transcendentals=0, bytes_accessed=8 * total * length
        ),
        name="rotate_step",
    )(me, rot_hi, rot_lo, hi, lo)


def place_kernel(me_ref, *refs, parts, offset):
    pieces = refs[:parts]
    out_ref, held_ref, sems = refs[-3:]
    me = me_ref[0]
    length = pieces[0].shape[1]
    loads = [pltpu.make_async_copy(pieces[t], held_ref.at[t], sems.at[0, t]) for t in range(parts)]
    for load in loads:
        load.start()
    stores = []
    for t in range(parts):
        loads[t].wait()
        at = pl.multiple_of(jnp.bitwise_xor(me, t) * length + offset, LANES)
        store = pltpu.make_async_copy(held_ref.at[t], out_ref.at[:, pl.ds(at, length)], sems.at[1, t])
        store.start()
        stores.append(store)
    for store in stores:
        store.wait()


def place_step(me, pieces, before, offset, shape):
    parts = len(pieces)
    anywhere = pl.BlockSpec(memory_space=pl.ANY)
    args = list(pieces) + ([] if before is None else [before])
    return pl.pallas_call(
        functools.partial(place_kernel, parts=parts, offset=offset),
        out_shape=jax.ShapeDtypeStruct(shape, jnp.float32),
        in_specs=[pl.BlockSpec(memory_space=pltpu.SMEM)] + [anywhere] * len(args),
        out_specs=anywhere,
        scratch_shapes=[
            pltpu.VMEM((parts,) + pieces[0].shape, jnp.float32),
            pltpu.SemaphoreType.DMA((2, parts)),
        ],
        input_output_aliases={} if before is None else {1 + parts: 0},
        name="place_step",
    )(me, *args)


def exchange(pieces, axis):
    count = len(pieces)
    return [pieces[0]] + [lax.ppermute(pieces[t], axis, [(i, i ^ t) for i in range(count)]) for t in range(1, count)]


def on_device(vectors, col_blocks, op_ids, coefficients, onsite, phonon_ops):
    vec_count, row_count = vectors.shape
    op_count, block_size = phonon_ops.shape[0], phonon_ops.shape[1]
    per_row = col_blocks.shape[1]
    block_count = row_count // block_size
    parts = lax.axis_size("vec")
    row_axis = lax.axis_size("row")
    bands = block_count // BAND
    if parts <= 8 and bands % 16 == 0 and (bands // 16 * BAND) % parts == 0:
        unit = bands // 16
        low_group, middle, high_group = (0, 3 * unit), (3 * unit, 8 * unit), (11 * unit, 5 * unit)
        order = [middle, high_group, low_group]
    else:
        order = [(0, bands)]
    me = lax.axis_index("vec").astype(jnp.int32)[None]
    first_block = lax.axis_index("row") * block_count
    upward = [(i, i + 1) for i in range(row_axis - 1)]
    downward = [(i + 1, i) for i in range(row_axis - 1)]

    def index_of(code):
        column = jnp.maximum(code // op_count - first_block + 2 * BAND, 0)
        return column % (RING * BAND) * op_count + code % op_count

    def with_ends(low_part, middle, high_part):
        return jnp.concatenate([low_part, middle, high_part])

    code = (col_blocks * op_count + op_ids).reshape(-1)
    coef = coefficients.reshape(-1)
    tail = BAND * per_row
    no_rows = jnp.zeros((tail,), jnp.int32)
    no_site = jnp.zeros((BAND * block_size,), jnp.float32)
    inner = (
        index_of(with_ends(no_rows, code, no_rows)),
        with_ends(no_site[:tail], coef, no_site[:tail]),
        with_ends(no_site, onsite, no_site)[None, :],
    )

    w_op = jnp.transpose(phonon_ops, (2, 0, 1)).reshape(block_size, op_count * block_size)
    w_high = lax.reduce_precision(w_op, 8, 7)
    w = jnp.concatenate([w_high, w_high, w_op - w_high], axis=0).astype(jnp.bfloat16)

    def first(table, start, count, low=None, high=None):
        return apply_ham(
            me, *table, w, vectors, max(start - 2, 0), count, start, start, start,
            low=low, high=high, op_count=op_count, per_row=per_row,
        )[0]

    def second(group, main, main_chunk, **kwargs):
        start, count = group
        part_blocks = count * BAND // parts
        return apply_ham(
            me, *inner, w, main, main_chunk, count, start + 1, start + 1, start + 1,
            base=vectors, base_chunk=start, parts=parts, part_blocks=part_blocks, op_count=op_count, per_row=per_row, **kwargs,
        )

    received = {}
    halo = 2 * BAND * block_size
    end_size = 2 * tail + BAND * block_size
    end_width = -(-end_size // (vec_count * LANES)) * LANES
    edges = []
    for a, b, c, d, e, f in (
        (code.shape[0] - tail, code.shape[0], row_count - BAND * block_size, row_count, row_count - halo, row_count),
        (0, tail, 0, BAND * block_size, 0, halo),
    ):
        end = jnp.concatenate([code[a:b].astype(jnp.float32), coef[a:b], onsite[c:d]])
        end = jnp.pad(end, (0, vec_count * end_width - end_size)).reshape(vec_count, end_width)
        edges.append(jnp.concatenate([vectors[:, e:f], end], axis=1))
    if len(order) > 1:
        step_mid = first(inner, middle[0], middle[1] + 2)
        step_mid, edges = lax.optimization_barrier((step_mid, edges))
    low_vectors = lax.ppermute(edges[0], "row", upward)
    high_vectors = lax.ppermute(edges[1], "row", downward)
    low_end = low_vectors[:, halo:].reshape(-1)[:end_size]
    high_end = high_vectors[:, halo:].reshape(-1)[:end_size]
    outer = (
        index_of(with_ends(low_end[:tail].astype(jnp.int32), code, high_end[:tail].astype(jnp.int32))),
        with_ends(low_end[tail : 2 * tail], coef, high_end[tail : 2 * tail]),
        with_ends(low_end[2 * tail :], onsite, high_end[2 * tail :])[None, :],
    )
    if len(order) == 1:
        steps = first(outer, 0, bands + 2, low=low_vectors, high=high_vectors)
        received[order[0]] = exchange(second(order[0], steps, 0), "vec")
    else:
        received[middle] = exchange(second(middle, step_mid, 0), "vec")
        step_high = first(outer, high_group[0] + 2, high_group[1], high=high_vectors)
        received[high_group] = exchange(
            second(high_group, step_high, 0, low=step_mid, low_chunk=middle[1]), "vec"
        )
        step_low = first(outer, 0, low_group[1], low=low_vectors)
        received[low_group] = exchange(second(low_group, step_low, 0, high=step_mid, high_chunk=0), "vec")

    stacks = {}
    partial_gram = None
    for place, group in enumerate(order):
        last = place + 1 == len(order)
        out = gram_step(me, received[group], partial_gram, last)
        stacks[group] = (out[0], out[1])
        partial_gram = out[2]
    mine = sum_of(exchange(out[2:], "vec"))
    summed = sum_of(
        [mine] + [lax.ppermute(mine, "row", [(i, i ^ k) for i in range(row_axis)]) for k in range(1, row_axis)]
    )
    shares = [summed] + [
        lax.ppermute(summed, "vec", [(i, i ^ t) for i in range(parts)]) for t in range(1, parts)
    ]
    rot_hi, rot_lo = inverse_of(me, shares, vec_count * parts, float(row_count * row_axis))

    result = None
    for group in order:
        pieces = exchange(rotate_step(me, rot_hi, rot_lo, *stacks[group], parts), "vec")
        result = place_step(me, pieces, result, group[0] * BAND * block_size, vectors.shape)
    return result


def solution(mesh):
    return jax.shard_map(
        on_device,
        mesh=mesh,
        in_specs=(P("vec", "row"), P("row", None), P("row", None), P("row", None), P("row"), P()),
        out_specs=P("vec", "row"),
        check_vma=False,
    )
```

```python
import functools

import jax
import jax.numpy as jnp
from jax import lax
from jax.experimental import pallas as pl
from jax.experimental.pallas import tpu as pltpu
from jax.sharding import PartitionSpec as P

BAND = 8
NS_ITERS = 3
CENTER = 0.25
HALF_WIDTH = 2.0
EPSILON = 1e-06
LANES = 128
RING = 3
VMEM_LIMIT = 58 * 1024 * 1024


def split(x):
    hi = x.astype(jnp.bfloat16)
    lo = (x - hi.astype(jnp.float32)).astype(jnp.bfloat16)
    return hi, lo


def dot(a, b):
    return jnp.dot(a, b, preferred_element_type=jnp.float32)


def ham_kernel(
    me_ref, idx_ref, coef_ref, *refs, steps, row_base, ring_base, op_count, per_row, has_low, has_high, second, parts, part_blocks
):
    refs = list(refs)
    main_ref = refs.pop(0)
    low_ref = refs.pop(0) if has_low else None
    high_ref = refs.pop(0) if has_high else None
    onsite_ref = refs.pop(0)
    base_ref = refs.pop(0) if second else None
    w_ref = refs.pop(0)
    outs = [refs.pop(0) for _ in range(parts if second else 1)]
    ring_ref = refs.pop(0)
    self_ref = refs.pop(0)
    stage_ref = refs.pop(0) if second else None
    i = pl.program_id(0)
    vec_count = main_ref.shape[0]
    source = main_ref[...]
    if has_low:
        source = jnp.where(i < 2, low_ref[...], source)
    if has_high:
        source = jnp.where(i >= steps - 2, high_ref[...], source)
    slot = lax.rem(i + ring_base, RING) * (BAND * op_count)
    x = jnp.concatenate([source[:, g * LANES : (g + 1) * LANES] for g in range(BAND)], axis=0)
    hi, lo = split(x)
    lhs = jnp.concatenate([hi, lo, hi], axis=1)
    for o in range(0, op_count, 2):
        t = dot(lhs, w_ref[:, o * LANES : (o + 2) * LANES])
        for g in range(BAND):
            for k in range(2):
                ring_ref[slot + g * op_count + o + k] = t[
                    g * vec_count : (g + 1) * vec_count, k * LANES : (k + 1) * LANES
                ]

    @pl.when(i >= 2)
    def _():
        previous = lax.rem(i + 1, 2)
        for g in range(BAND):
            block = (i - 2) * BAND + g
            row = (block + row_base) * per_row
            span = slice(g * LANES, (g + 1) * LANES)
            own = self_ref[previous, :, span]
            acc = (onsite_ref[:, span] - CENTER) * own
            for j in range(per_row):
                acc = acc + coef_ref[row + j] * ring_ref[idx_ref[row + j]]
            if second:
                acc = acc - base_ref[:, span]
                peer = lax.div(block, part_blocks)
                place = jnp.bitwise_xor(peer, me_ref[0]) * part_blocks + lax.rem(block, part_blocks)
                stage_ref[place] = acc
            else:
                outs[0][:, span] = acc * (1.0 / HALF_WIDTH)

    self_ref[lax.rem(i, 2)] = source
    if second:

        @pl.when(i == steps - 1)
        def _():
            for part in range(parts):
                for s in range(part_blocks):
                    outs[part][:, s * LANES : (s + 1) * LANES] = stage_ref[part * part_blocks + s]


def apply_ham(
    me, idx, coef, onsite, w, main, main_chunk, chunks, row_chunk, ring_base, onsite_chunk,
    low=None, low_chunk=0, high=None, high_chunk=0, base=None, base_chunk=0, parts=0, part_blocks=1, op_count=16, per_row=16,
):
    vec_count = main.shape[0]
    width = BAND * LANES
    steps = chunks + 2
    second = base is not None
    main_first = 2 if low is not None else 0
    main_last = steps - 1 - (2 if high is not None else 0)
    spec = functools.partial(pl.BlockSpec, (vec_count, width))
    in_specs = [spec(lambda i, *_: (0, jnp.clip(i, main_first, main_last) - main_first + main_chunk))]
    args = [main]
    if low is not None:
        in_specs.append(spec(lambda i, *_: (0, jnp.clip(i, 0, 1) + low_chunk)))
        args.append(low)
    if high is not None:
        in_specs.append(spec(lambda i, *_: (0, jnp.clip(i - (steps - 2), 0, 1) + high_chunk)))
        args.append(high)
    in_specs.append(pl.BlockSpec((1, width), lambda i, *_: (0, jnp.maximum(i - 2, 0) + onsite_chunk)))
    args.append(onsite)
    if second:
        in_specs.append(spec(lambda i, *_: (0, jnp.maximum(i - 2, 0) + base_chunk)))
        args.append(base)
    in_specs.append(pl.BlockSpec(w.shape, lambda i, *_: (0, 0)))
    args.append(w)
    scratch = [
        pltpu.VMEM((RING * BAND * op_count, vec_count, LANES), jnp.float32),
        pltpu.VMEM((2, vec_count, width), jnp.float32),
    ]
    if second:
        out_shape = [jax.ShapeDtypeStruct((vec_count, part_blocks * LANES), jnp.float32)] * parts
        out_specs = [pl.BlockSpec((vec_count, part_blocks * LANES), lambda i, *_: (0, 0))] * parts
        scratch.append(pltpu.VMEM((parts * part_blocks, vec_count, LANES), jnp.float32))
    else:
        out_shape = [jax.ShapeDtypeStruct((vec_count, chunks * width), jnp.float32)]
        out_specs = [spec(lambda i, *_: (0, jnp.maximum(i - 2, 0)))]
    flops = 2 * steps * BAND * vec_count * 3 * LANES * LANES * op_count
    return pl.pallas_call(
        functools.partial(
            ham_kernel,
            steps=steps,
            row_base=row_chunk * BAND,
            ring_base=ring_base,
            op_count=op_count,
            per_row=per_row,
            has_low=low is not None,
            has_high=high is not None,
            second=second,
            parts=parts,
            part_blocks=part_blocks,
        ),
        out_shape=out_shape,
        grid_spec=pltpu.PrefetchScalarGridSpec(
            num_scalar_prefetch=3, grid=(steps,), in_specs=in_specs, out_specs=out_specs, scratch_shapes=scratch
        ),
        compiler_params=pltpu.CompilerParams(vmem_limit_bytes=VMEM_LIMIT),
        cost_estimate=pl.CostEstimate(flops=2 * flops, transcendentals=0, bytes_accessed=8 * steps * vec_count * width),
        name="ham_second" if second else "ham_first",
    )(me, idx, coef, *args)


def gram_kernel(me_ref, *refs, parts, sets, first, last):
    refs = list(refs)
    groups = [[refs.pop(0) for _ in range(parts)] for _ in range(sets)]
    before_ref = None if first else refs.pop(0)
    stacks = [(refs.pop(0), refs.pop(0)) for _ in range(sets)]
    outs = [refs.pop(0) for _ in range(parts if last else 1)]
    stage_ref = refs.pop(0)
    me = me_ref[0]
    vec_count = groups[0][0].shape[0]
    total = parts * vec_count
    contract = (((1,), (1,)), ((), ()))
    for number, (pieces, (hi_ref, lo_ref)) in enumerate(zip(groups, stacks)):
        for t in range(parts):
            place = pl.multiple_of(jnp.bitwise_xor(me, t) * vec_count, vec_count)
            hi, lo = split(pieces[t][...])
            hi_ref[pl.ds(place, vec_count), :] = hi
            lo_ref[pl.ds(place, vec_count), :] = lo
        hi, lo = hi_ref[...], lo_ref[...]
        square = lax.dot_general(hi, hi, contract, preferred_element_type=jnp.float32)
        cross = lax.dot_general(hi, lo, contract, preferred_element_type=jnp.float32)
        if number > 0:
            stage_ref[0] += square
            stage_ref[1] += cross
        elif first:
            stage_ref[0] = square
            stage_ref[1] = cross
        else:
            stage_ref[0] = before_ref[0] + square
            stage_ref[1] = before_ref[1] + cross
    if not last:
        outs[0][...] = stage_ref[...]
    else:
        packed_ref = refs.pop(0)
        tile = total // 4
        at = 0
        for left in range(4):
            for right in range(left, 4):
                a = slice(left * tile, (left + 1) * tile)
                b = slice(right * tile, (right + 1) * tile)
                packed_ref[at * tile : (at + 1) * tile, :] = (
                    stage_ref[0, a, b] + stage_ref[1, a, b] + stage_ref[1, b, a].T
                )
                at += 1
        rows = at * tile // parts
        for t in range(parts):
            place = pl.multiple_of(jnp.bitwise_xor(me, t) * rows, 8)
            outs[t][...] = packed_ref[pl.ds(place, rows), :]


def gram_step(me, groups, before, last):
    parts = len(groups[0])
    vec_count = groups[0][0].shape[0]
    lengths = [pieces[0].shape[1] for pieces in groups]
    total = parts * vec_count
    stacks = [jax.ShapeDtypeStruct((total, length), jnp.bfloat16) for length in lengths for _ in range(2)]
    length = sum(lengths)
    tile = total // 4
    if last:
        outs = [jax.ShapeDtypeStruct((10 * tile // parts, tile), jnp.float32)] * parts
        extra = [pltpu.VMEM((10 * tile, tile), jnp.float32)]
    else:
        outs = [jax.ShapeDtypeStruct((2, total, total), jnp.float32)]
        extra = []
    vmem = pl.BlockSpec(memory_space=pltpu.VMEM)
    args = [piece for pieces in groups for piece in pieces] + ([] if before is None else [before])
    return pl.pallas_call(
        functools.partial(gram_kernel, parts=parts, sets=len(groups), first=before is None, last=last),
        out_shape=stacks + outs,
        in_specs=[pl.BlockSpec(memory_space=pltpu.SMEM)] + [vmem] * len(args),
        out_specs=[vmem] * (len(stacks) + len(outs)),
        scratch_shapes=[pltpu.VMEM((2, total, total), jnp.float32)] + extra,
        compiler_params=pltpu.CompilerParams(vmem_limit_bytes=VMEM_LIMIT),
        cost_estimate=pl.CostEstimate(
            flops=4 * total * total * length, transcendentals=0, bytes_accessed=8 * total * length
        ),
        name="gram_step",
    )(me, *args)


def sum_kernel(*refs):
    acc = refs[0][...]
    for ref in refs[1:-1]:
        acc = acc + ref[...]
    refs[-1][...] = acc


def sum_of(arrays):
    return pl.pallas_call(
        sum_kernel, out_shape=jax.ShapeDtypeStruct(arrays[0].shape, jnp.float32), name="sum_of"
    )(*arrays)


def inverse_kernel(me_ref, *refs, parts, total, scale_rows):
    pieces = refs[:parts]
    hi_ref, lo_ref, packed_ref, gram_ref = refs[parts:]
    me = me_ref[0]
    rows = pieces[0].shape[0]
    for t in range(parts):
        place = pl.multiple_of(jnp.bitwise_xor(me, t) * rows, 8)
        packed_ref[pl.ds(place, rows), :] = pieces[t][...]
    tile = total // 4
    at = 0
    for left in range(4):
        for right in range(left, 4):
            block = packed_ref[at * tile : (at + 1) * tile, :]
            a = slice(left * tile, (left + 1) * tile)
            b = slice(right * tile, (right + 1) * tile)
            gram_ref[a, b] = block
            if left != right:
                gram_ref[b, a] = block.T
            at += 1
    gram = gram_ref[...]
    gram_norm = jnp.sqrt(jnp.sum(gram * gram, keepdims=True) + EPSILON)
    eye = (
        lax.broadcasted_iota(jnp.int32, (total, total), 0) == lax.broadcasted_iota(jnp.int32, (total, total), 1)
    ).astype(jnp.float32)

    def mul(a, b):
        ah, al = split(a)
        bh, bl = split(b)
        return dot(ah, bh) + (dot(ah, bl) + dot(al, bh))

    approx = gram / gram_norm
    inverse = None
    for step in range(NS_ITERS):
        product = approx if inverse is None else mul(inverse, approx)
        correction = (3.0 * eye - product) * 0.5
        if step + 1 < NS_ITERS:
            approx = mul(approx, correction)
        inverse = correction if inverse is None else mul(correction, inverse)
    rotation = inverse.T * jnp.sqrt(scale_rows / gram_norm)
    hi, lo = split(rotation)
    hi_ref[...] = hi
    lo_ref[...] = lo


def inverse_of(me, pieces, total, scale_rows):
    parts = len(pieces)
    tile = total // 4
    vmem = pl.BlockSpec(memory_space=pltpu.VMEM)
    return pl.pallas_call(
        functools.partial(inverse_kernel, parts=parts, total=total, scale_rows=scale_rows),
        out_shape=[jax.ShapeDtypeStruct((total, total), jnp.bfloat16)] * 2,
        in_specs=[pl.BlockSpec(memory_space=pltpu.SMEM)] + [vmem] * parts,
        out_specs=[vmem] * 2,
        scratch_shapes=[pltpu.VMEM((10 * tile, tile), jnp.float32), pltpu.VMEM((total, total), jnp.float32)],
        compiler_params=pltpu.CompilerParams(vmem_limit_bytes=VMEM_LIMIT),
        name="inverse_of",
    )(me, *pieces)


def rotate_kernel(me_ref, rh_ref, rl_ref, hi_ref, lo_ref, *refs, parts):
    outs, stage_ref = refs[:parts], refs[parts]
    me = me_ref[0]
    vec_count = outs[0].shape[0]
    hi, lo = hi_ref[...], lo_ref[...]
    stage_ref[...] = dot(rh_ref[...], hi) + (dot(rh_ref[...], lo) + dot(rl_ref[...], hi))
    for t in range(parts):
        place = pl.multiple_of(jnp.bitwise_xor(me, t) * vec_count, vec_count)
        outs[t][...] = stage_ref[pl.ds(place, vec_count), :]


def rotate_step(me, rot_hi, rot_lo, hi, lo, parts, cut, cuts):
    total, length = hi.shape[0], hi.shape[1] // cuts
    vmem = pl.BlockSpec(memory_space=pltpu.VMEM)
    return pl.pallas_call(
        functools.partial(rotate_kernel, parts=parts),
        out_shape=[jax.ShapeDtypeStruct((total // parts, length), jnp.float32)] * parts,
        grid=(1,),
        in_specs=[pl.BlockSpec(memory_space=pltpu.SMEM)]
        + [pl.BlockSpec((total, total), lambda i: (0, 0))] * 2
        + [pl.BlockSpec((total, length), lambda i: (0, cut))] * 2,
        out_specs=[vmem] * parts,
        scratch_shapes=[pltpu.VMEM((total, length), jnp.float32)],
        compiler_params=pltpu.CompilerParams(vmem_limit_bytes=VMEM_LIMIT),
        cost_estimate=pl.CostEstimate(
            flops=6 * total * total * length, transcendentals=0, bytes_accessed=8 * total * length
        ),
        name="rotate_step",
    )(me, rot_hi, rot_lo, hi, lo)


def place_kernel(me_ref, *refs, parts, offset, stride):
    pieces = refs[:parts]
    out_ref, held_ref, sems = refs[-3:]
    me = me_ref[0]
    length = pieces[0].shape[1]
    loads = [pltpu.make_async_copy(pieces[t], held_ref.at[t], sems.at[0, t]) for t in range(parts)]
    for load in loads:
        load.start()
    stores = []
    for t in range(parts):
        loads[t].wait()
        at = pl.multiple_of(jnp.bitwise_xor(me, t) * stride + offset, LANES)
        store = pltpu.make_async_copy(held_ref.at[t], out_ref.at[:, pl.ds(at, length)], sems.at[1, t])
        store.start()
        stores.append(store)
    for store in stores:
        store.wait()


def place_step(me, pieces, before, offset, stride, shape):
    parts = len(pieces)
    anywhere = pl.BlockSpec(memory_space=pl.ANY)
    args = list(pieces) + ([] if before is None else [before])
    return pl.pallas_call(
        functools.partial(place_kernel, parts=parts, offset=offset, stride=stride),
        out_shape=jax.ShapeDtypeStruct(shape, jnp.float32),
        in_specs=[pl.BlockSpec(memory_space=pltpu.SMEM)] + [anywhere] * len(args),
        out_specs=anywhere,
        scratch_shapes=[
            pltpu.VMEM((parts,) + pieces[0].shape, jnp.float32),
            pltpu.SemaphoreType.DMA((2, parts)),
        ],
        input_output_aliases={} if before is None else {1 + parts: 0},
        name="place_step",
    )(me, *args)


def exchange(pieces, axis):
    count = len(pieces)
    return [pieces[0]] + [lax.ppermute(pieces[t], axis, [(i, i ^ t) for i in range(count)]) for t in range(1, count)]


def on_device(vectors, col_blocks, op_ids, coefficients, onsite, phonon_ops):
    vec_count, row_count = vectors.shape
    op_count, block_size = phonon_ops.shape[0], phonon_ops.shape[1]
    per_row = col_blocks.shape[1]
    block_count = row_count // block_size
    parts = lax.axis_size("vec")
    row_axis = lax.axis_size("row")
    bands = block_count // BAND
    if parts <= 8 and bands % 16 == 0 and (bands // 16 * BAND) % parts == 0:
        unit = bands // 16
        low_group, middle, high_group = (0, 3 * unit), (3 * unit, 8 * unit), (11 * unit, 5 * unit)
        order = [middle, high_group, low_group]
    else:
        order = [(0, bands)]
    me = lax.axis_index("vec").astype(jnp.int32)[None]
    first_block = lax.axis_index("row") * block_count
    upward = [(i, i + 1) for i in range(row_axis - 1)]
    downward = [(i + 1, i) for i in range(row_axis - 1)]

    def index_of(code):
        column = jnp.maximum(code // op_count - first_block + 2 * BAND, 0)
        return column % (RING * BAND) * op_count + code % op_count

    def with_ends(low_part, middle, high_part):
        return jnp.concatenate([low_part, middle, high_part])

    code = (col_blocks * op_count + op_ids).reshape(-1)
    coef = coefficients.reshape(-1)
    tail = BAND * per_row
    no_rows = jnp.zeros((tail,), jnp.int32)
    no_site = jnp.zeros((tail,), jnp.float32)
    inner = (
        index_of(with_ends(no_rows, code, no_rows)),
        with_ends(no_site, coef, no_site),
        onsite[None, :],
    )

    w_op = jnp.transpose(phonon_ops, (2, 0, 1)).reshape(block_size, op_count * block_size)
    w_high = lax.reduce_precision(w_op, 8, 7)
    w = jnp.concatenate([w_high, w_high, w_op - w_high], axis=0).astype(jnp.bfloat16)

    def first(table, start, count, low=None, high=None):
        return apply_ham(
            me, *table, w, vectors, max(start - 2, 0), count, start, start, start - 1 if table is inner else start,
            low=low, high=high, op_count=op_count, per_row=per_row,
        )[0]

    def second(group, main, main_chunk, **kwargs):
        start, count = group
        part_blocks = count * BAND // parts
        return apply_ham(
            me, *inner, w, main, main_chunk, count, start + 1, start + 1, start,
            base=vectors, base_chunk=start, parts=parts, part_blocks=part_blocks, op_count=op_count, per_row=per_row, **kwargs,
        )

    received = {}
    halo = 2 * BAND * block_size
    end_size = 2 * tail + BAND * block_size
    end_width = -(-end_size // (vec_count * LANES)) * LANES
    edges = []
    for a, b, c, d, e, f in (
        (code.shape[0] - tail, code.shape[0], row_count - BAND * block_size, row_count, row_count - halo, row_count),
        (0, tail, 0, BAND * block_size, 0, halo),
    ):
        end = jnp.concatenate([code[a:b].astype(jnp.float32), coef[a:b], onsite[c:d]])
        end = jnp.pad(end, (0, vec_count * end_width - end_size)).reshape(vec_count, end_width)
        edges.append(jnp.concatenate([vectors[:, e:f], end], axis=1))
    if len(order) > 1:
        step_mid = first(inner, middle[0], middle[1] + 2)
        step_mid, edges = lax.optimization_barrier((step_mid, edges))
    low_vectors = lax.ppermute(edges[0], "row", upward)
    high_vectors = lax.ppermute(edges[1], "row", downward)
    low_end = low_vectors[:, halo:].reshape(-1)[:end_size]
    high_end = high_vectors[:, halo:].reshape(-1)[:end_size]
    outer = (
        index_of(with_ends(low_end[:tail].astype(jnp.int32), code, high_end[:tail].astype(jnp.int32))),
        with_ends(low_end[tail : 2 * tail], coef, high_end[tail : 2 * tail]),
        with_ends(low_end[2 * tail :], onsite, high_end[2 * tail :])[None, :],
    )
    if len(order) == 1:
        steps = first(outer, 0, bands + 2, low=low_vectors, high=high_vectors)
        received[order[0]] = exchange(second(order[0], steps, 0), "vec")
    else:
        received[middle] = exchange(second(middle, step_mid, 0), "vec")
        step_high = first(outer, high_group[0] + 2, high_group[1], high=high_vectors)
        received[high_group] = exchange(
            second(high_group, step_high, 0, low=step_mid, low_chunk=middle[1]), "vec"
        )
        step_low = first(outer, 0, low_group[1], low=low_vectors)
        received[low_group] = exchange(second(low_group, step_low, 0, high=step_mid, high_chunk=0), "vec")

    stacks = {}
    before = None
    for batch in (order[:-1], order[-1:]):
        if batch:
            out = gram_step(me, [received[group] for group in batch], before, batch[-1] == order[-1])
            for number, group in enumerate(batch):
                stacks[group] = out[2 * number : 2 * number + 2]
            out = out[2 * len(batch) :]
            before = out[0]
    mine = sum_of(exchange(out, "vec"))
    summed = sum_of(
        [mine] + [lax.ppermute(mine, "row", [(i, i ^ k) for i in range(row_axis)]) for k in range(1, row_axis)]
    )
    shares = [summed] + [
        lax.ppermute(summed, "vec", [(i, i ^ t) for i in range(parts)]) for t in range(1, parts)
    ]
    rot_hi, rot_lo = inverse_of(me, shares, vec_count * parts, float(row_count * row_axis))

    result = None
    for group in order:
        stride = group[1] * BAND * block_size // parts
        cuts = 2 if len(order) > 1 and group == middle else 1
        for cut in range(cuts):
            pieces = exchange(rotate_step(me, rot_hi, rot_lo, *stacks[group], parts, cut, cuts), "vec")
            offset = group[0] * BAND * block_size + cut * (stride // cuts)
            result = place_step(me, pieces, result, offset, stride, vectors.shape)
    return result


def solution(mesh):
    return jax.shard_map(
        on_device,
        mesh=mesh,
        in_specs=(P("vec", "row"), P("row", None), P("row", None), P("row", None), P("row"), P()),
        out_specs=P("vec", "row"),
        check_vma=False,
    )
```

```python
import functools

import jax
import jax.numpy as jnp
from jax import lax
from jax.experimental import pallas as pl
from jax.experimental.pallas import tpu as pltpu
from jax.sharding import PartitionSpec as P

BAND = 8
NS_ITERS = 3
CENTER = 0.25
HALF_WIDTH = 2.0
EPSILON = 1e-06
LANES = 128
RING = 3
VMEM_LIMIT = 58 * 1024 * 1024


def split(x):
    hi = x.astype(jnp.bfloat16)
    lo = (x - hi.astype(jnp.float32)).astype(jnp.bfloat16)
    return hi, lo


def dot(a, b):
    return jnp.dot(a, b, preferred_element_type=jnp.float32)


def ham_kernel(
    me_ref, idx_ref, coef_ref, *refs, steps, row_base, ring_base, op_count, per_row, has_low, has_high, second, parts, part_blocks
):
    refs = list(refs)
    main_ref = refs.pop(0)
    low_ref = refs.pop(0) if has_low else None
    high_ref = refs.pop(0) if has_high else None
    onsite_ref = refs.pop(0)
    base_ref = refs.pop(0) if second else None
    w_ref = refs.pop(0)
    outs = [refs.pop(0) for _ in range(parts if second else 1)]
    ring_ref = refs.pop(0)
    self_ref = refs.pop(0)
    stage_ref = refs.pop(0) if second else None
    i = pl.program_id(0)
    vec_count = main_ref.shape[0]
    source = main_ref[...]
    if has_low:
        source = jnp.where(i < 2, low_ref[...], source)
    if has_high:
        source = jnp.where(i >= steps - 2, high_ref[...], source)
    slot = lax.rem(i + ring_base, RING) * (BAND * op_count)
    x = jnp.concatenate([source[:, g * LANES : (g + 1) * LANES] for g in range(BAND)], axis=0)
    hi, lo = split(x)
    lhs = jnp.concatenate([hi, lo, hi], axis=1)
    for o in range(0, op_count, 2):
        t = dot(lhs, w_ref[:, o * LANES : (o + 2) * LANES])
        for g in range(BAND):
            for k in range(2):
                ring_ref[slot + g * op_count + o + k] = t[
                    g * vec_count : (g + 1) * vec_count, k * LANES : (k + 1) * LANES
                ]

    @pl.when(i >= 2)
    def _():
        previous = lax.rem(i + 1, 2)
        for g in range(BAND):
            block = (i - 2) * BAND + g
            row = (block + row_base) * per_row
            span = slice(g * LANES, (g + 1) * LANES)
            own = self_ref[previous, :, span]
            acc = (onsite_ref[:, span] - CENTER) * own
            for j in range(per_row):
                acc = acc + coef_ref[row + j] * ring_ref[idx_ref[row + j]]
            if second:
                acc = acc - base_ref[:, span]
                peer = lax.div(block, part_blocks)
                place = jnp.bitwise_xor(peer, me_ref[0]) * part_blocks + lax.rem(block, part_blocks)
                stage_ref[place] = acc
            else:
                outs[0][:, span] = acc * (1.0 / HALF_WIDTH)

    self_ref[lax.rem(i, 2)] = source
    if second:

        @pl.when(i == steps - 1)
        def _():
            for part in range(parts):
                for s in range(part_blocks):
                    outs[part][:, s * LANES : (s + 1) * LANES] = stage_ref[part * part_blocks + s]


def apply_ham(
    me, idx, coef, onsite, w, main, main_chunk, chunks, row_chunk, ring_base, onsite_chunk,
    low=None, low_chunk=0, high=None, high_chunk=0, base=None, base_chunk=0, parts=0, part_blocks=1, op_count=16, per_row=16,
):
    vec_count = main.shape[0]
    width = BAND * LANES
    steps = chunks + 2
    second = base is not None
    main_first = 2 if low is not None else 0
    main_last = steps - 1 - (2 if high is not None else 0)
    spec = functools.partial(pl.BlockSpec, (vec_count, width))
    in_specs = [spec(lambda i, *_: (0, jnp.clip(i, main_first, main_last) - main_first + main_chunk))]
    args = [main]
    if low is not None:
        in_specs.append(spec(lambda i, *_: (0, jnp.clip(i, 0, 1) + low_chunk)))
        args.append(low)
    if high is not None:
        in_specs.append(spec(lambda i, *_: (0, jnp.clip(i - (steps - 2), 0, 1) + high_chunk)))
        args.append(high)
    in_specs.append(pl.BlockSpec((1, width), lambda i, *_: (0, jnp.maximum(i - 2, 0) + onsite_chunk)))
    args.append(onsite)
    if second:
        in_specs.append(spec(lambda i, *_: (0, jnp.maximum(i - 2, 0) + base_chunk)))
        args.append(base)
    in_specs.append(pl.BlockSpec(w.shape, lambda i, *_: (0, 0)))
    args.append(w)
    scratch = [
        pltpu.VMEM((RING * BAND * op_count, vec_count, LANES), jnp.float32),
        pltpu.VMEM((2, vec_count, width), jnp.float32),
    ]
    if second:
        out_shape = [jax.ShapeDtypeStruct((vec_count, part_blocks * LANES), jnp.float32)] * parts
        out_specs = [pl.BlockSpec((vec_count, part_blocks * LANES), lambda i, *_: (0, 0))] * parts
        scratch.append(pltpu.VMEM((parts * part_blocks, vec_count, LANES), jnp.float32))
    else:
        out_shape = [jax.ShapeDtypeStruct((vec_count, chunks * width), jnp.float32)]
        out_specs = [spec(lambda i, *_: (0, jnp.maximum(i - 2, 0)))]
    flops = 2 * steps * BAND * vec_count * 3 * LANES * LANES * op_count
    return pl.pallas_call(
        functools.partial(
            ham_kernel,
            steps=steps,
            row_base=row_chunk * BAND,
            ring_base=ring_base,
            op_count=op_count,
            per_row=per_row,
            has_low=low is not None,
            has_high=high is not None,
            second=second,
            parts=parts,
            part_blocks=part_blocks,
        ),
        out_shape=out_shape,
        grid_spec=pltpu.PrefetchScalarGridSpec(
            num_scalar_prefetch=3, grid=(steps,), in_specs=in_specs, out_specs=out_specs, scratch_shapes=scratch
        ),
        compiler_params=pltpu.CompilerParams(vmem_limit_bytes=VMEM_LIMIT),
        cost_estimate=pl.CostEstimate(flops=2 * flops, transcendentals=0, bytes_accessed=8 * steps * vec_count * width),
        name="ham_second" if second else "ham_first",
    )(me, idx, coef, *args)


def gram_kernel(me_ref, *refs, parts, sets, first, last):
    refs = list(refs)
    groups = [[refs.pop(0) for _ in range(parts)] for _ in range(sets)]
    before_ref = None if first else refs.pop(0)
    stacks = [(refs.pop(0), refs.pop(0)) for _ in range(sets)]
    outs = [refs.pop(0) for _ in range(parts if last else 1)]
    stage_ref = refs.pop(0)
    me = me_ref[0]
    vec_count = groups[0][0].shape[0]
    total = parts * vec_count
    contract = (((1,), (1,)), ((), ()))
    for number, (pieces, (hi_ref, lo_ref)) in enumerate(zip(groups, stacks)):
        for t in range(parts):
            place = pl.multiple_of(jnp.bitwise_xor(me, t) * vec_count, vec_count)
            hi, lo = split(pieces[t][...])
            hi_ref[pl.ds(place, vec_count), :] = hi
            lo_ref[pl.ds(place, vec_count), :] = lo
        hi, lo = hi_ref[...], lo_ref[...]
        square = lax.dot_general(hi, hi, contract, preferred_element_type=jnp.float32)
        cross = lax.dot_general(hi, lo, contract, preferred_element_type=jnp.float32)
        if number > 0:
            stage_ref[0] += square
            stage_ref[1] += cross
        elif first:
            stage_ref[0] = square
            stage_ref[1] = cross
        else:
            stage_ref[0] = before_ref[0] + square
            stage_ref[1] = before_ref[1] + cross
    if not last:
        outs[0][...] = stage_ref[...]
    else:
        packed_ref = refs.pop(0)
        tile = total // 4
        at = 0
        for left in range(4):
            for right in range(left, 4):
                a = slice(left * tile, (left + 1) * tile)
                b = slice(right * tile, (right + 1) * tile)
                packed_ref[at * tile : (at + 1) * tile, :] = (
                    stage_ref[0, a, b] + stage_ref[1, a, b] + stage_ref[1, b, a].T
                )
                at += 1
        rows = at * tile // parts
        for t in range(parts):
            place = pl.multiple_of(jnp.bitwise_xor(me, t) * rows, 8)
            outs[t][...] = packed_ref[pl.ds(place, rows), :]


def gram_step(me, groups, before, last):
    parts = len(groups[0])
    vec_count = groups[0][0].shape[0]
    lengths = [pieces[0].shape[1] for pieces in groups]
    total = parts * vec_count
    stacks = [jax.ShapeDtypeStruct((total, length), jnp.bfloat16) for length in lengths for _ in range(2)]
    length = sum(lengths)
    tile = total // 4
    if last:
        outs = [jax.ShapeDtypeStruct((10 * tile // parts, tile), jnp.float32)] * parts
        extra = [pltpu.VMEM((10 * tile, tile), jnp.float32)]
    else:
        outs = [jax.ShapeDtypeStruct((2, total, total), jnp.float32)]
        extra = []
    vmem = pl.BlockSpec(memory_space=pltpu.VMEM)
    args = [piece for pieces in groups for piece in pieces] + ([] if before is None else [before])
    return pl.pallas_call(
        functools.partial(gram_kernel, parts=parts, sets=len(groups), first=before is None, last=last),
        out_shape=stacks + outs,
        in_specs=[pl.BlockSpec(memory_space=pltpu.SMEM)] + [vmem] * len(args),
        out_specs=[vmem] * (len(stacks) + len(outs)),
        scratch_shapes=[pltpu.VMEM((2, total, total), jnp.float32)] + extra,
        compiler_params=pltpu.CompilerParams(vmem_limit_bytes=VMEM_LIMIT),
        cost_estimate=pl.CostEstimate(
            flops=4 * total * total * length, transcendentals=0, bytes_accessed=8 * total * length
        ),
        name="gram_step",
    )(me, *args)


def sum_kernel(*refs):
    acc = refs[0][...]
    for ref in refs[1:-1]:
        acc = acc + ref[...]
    refs[-1][...] = acc


def sum_of(arrays):
    return pl.pallas_call(
        sum_kernel, out_shape=jax.ShapeDtypeStruct(arrays[0].shape, jnp.float32), name="sum_of"
    )(*arrays)


def inverse_kernel(me_ref, *refs, parts, total, scale_rows):
    pieces = refs[:parts]
    hi_ref, lo_ref, packed_ref, gram_ref = refs[parts:]
    me = me_ref[0]
    rows = pieces[0].shape[0]
    for t in range(parts):
        place = pl.multiple_of(jnp.bitwise_xor(me, t) * rows, 8)
        packed_ref[pl.ds(place, rows), :] = pieces[t][...]
    tile = total // 4
    at = 0
    for left in range(4):
        for right in range(left, 4):
            block = packed_ref[at * tile : (at + 1) * tile, :]
            a = slice(left * tile, (left + 1) * tile)
            b = slice(right * tile, (right + 1) * tile)
            gram_ref[a, b] = block
            if left != right:
                gram_ref[b, a] = block.T
            at += 1
    gram = gram_ref[...]
    gram_norm = jnp.sqrt(jnp.sum(gram * gram, keepdims=True) + EPSILON)
    eye = (
        lax.broadcasted_iota(jnp.int32, (total, total), 0) == lax.broadcasted_iota(jnp.int32, (total, total), 1)
    ).astype(jnp.float32)

    def mul(a, b):
        ah, al = split(a)
        bh, bl = split(b)
        return dot(ah, bh) + (dot(ah, bl) + dot(al, bh))

    approx = gram / gram_norm
    inverse = None
    for step in range(NS_ITERS):
        product = approx if inverse is None else mul(inverse, approx)
        correction = (3.0 * eye - product) * 0.5
        if step + 1 < NS_ITERS:
            approx = mul(approx, correction)
        inverse = correction if inverse is None else mul(correction, inverse)
    rotation = inverse.T * jnp.sqrt(scale_rows / gram_norm)
    hi, lo = split(rotation)
    hi_ref[...] = hi
    lo_ref[...] = lo


def inverse_of(me, pieces, total, scale_rows):
    parts = len(pieces)
    tile = total // 4
    vmem = pl.BlockSpec(memory_space=pltpu.VMEM)
    return pl.pallas_call(
        functools.partial(inverse_kernel, parts=parts, total=total, scale_rows=scale_rows),
        out_shape=[jax.ShapeDtypeStruct((total, total), jnp.bfloat16)] * 2,
        in_specs=[pl.BlockSpec(memory_space=pltpu.SMEM)] + [vmem] * parts,
        out_specs=[vmem] * 2,
        scratch_shapes=[pltpu.VMEM((10 * tile, tile), jnp.float32), pltpu.VMEM((total, total), jnp.float32)],
        compiler_params=pltpu.CompilerParams(vmem_limit_bytes=VMEM_LIMIT),
        name="inverse_of",
    )(me, *pieces)


def rotate_kernel(me_ref, rh_ref, rl_ref, hi_ref, lo_ref, *refs, parts):
    outs, stage_ref = refs[:parts], refs[parts]
    me = me_ref[0]
    vec_count = outs[0].shape[0]
    hi, lo = hi_ref[...], lo_ref[...]
    stage_ref[...] = dot(rh_ref[...], hi) + (dot(rh_ref[...], lo) + dot(rl_ref[...], hi))
    for t in range(parts):
        place = pl.multiple_of(jnp.bitwise_xor(me, t) * vec_count, vec_count)
        outs[t][...] = stage_ref[pl.ds(place, vec_count), :]


def rotate_step(me, rot_hi, rot_lo, hi, lo, parts, cut, cuts):
    total, length = hi.shape[0], hi.shape[1] // cuts
    vmem = pl.BlockSpec(memory_space=pltpu.VMEM)
    return pl.pallas_call(
        functools.partial(rotate_kernel, parts=parts),
        out_shape=[jax.ShapeDtypeStruct((total // parts, length), jnp.float32)] * parts,
        grid=(1,),
        in_specs=[pl.BlockSpec(memory_space=pltpu.SMEM)]
        + [pl.BlockSpec((total, total), lambda i: (0, 0))] * 2
        + [pl.BlockSpec((total, length), lambda i: (0, cut))] * 2,
        out_specs=[vmem] * parts,
        scratch_shapes=[pltpu.VMEM((total, length), jnp.float32)],
        compiler_params=pltpu.CompilerParams(vmem_limit_bytes=VMEM_LIMIT),
        cost_estimate=pl.CostEstimate(
            flops=6 * total * total * length, transcendentals=0, bytes_accessed=8 * total * length
        ),
        name="rotate_step",
    )(me, rot_hi, rot_lo, hi, lo)


def place_kernel(me_ref, *refs, parts, offset, stride):
    pieces = refs[:parts]
    out_ref, held_ref, sems = refs[-3:]
    me = me_ref[0]
    length = pieces[0].shape[1]
    loads = [pltpu.make_async_copy(pieces[t], held_ref.at[t], sems.at[0, t]) for t in range(parts)]
    for load in loads:
        load.start()
    stores = []
    for t in range(parts):
        loads[t].wait()
        at = pl.multiple_of(jnp.bitwise_xor(me, t) * stride + offset, LANES)
        store = pltpu.make_async_copy(held_ref.at[t], out_ref.at[:, pl.ds(at, length)], sems.at[1, t])
        store.start()
        stores.append(store)
    for store in stores:
        store.wait()


def place_step(me, pieces, before, offset, stride, shape):
    parts = len(pieces)
    anywhere = pl.BlockSpec(memory_space=pl.ANY)
    args = list(pieces) + ([] if before is None else [before])
    return pl.pallas_call(
        functools.partial(place_kernel, parts=parts, offset=offset, stride=stride),
        out_shape=jax.ShapeDtypeStruct(shape, jnp.float32),
        in_specs=[pl.BlockSpec(memory_space=pltpu.SMEM)] + [anywhere] * len(args),
        out_specs=anywhere,
        scratch_shapes=[
            pltpu.VMEM((parts,) + pieces[0].shape, jnp.float32),
            pltpu.SemaphoreType.DMA((2, parts)),
        ],
        input_output_aliases={} if before is None else {1 + parts: 0},
        name="place_step",
    )(me, *args)


def exchange(pieces, axis):
    count = len(pieces)
    return [pieces[0]] + [lax.ppermute(pieces[t], axis, [(i, i ^ t) for i in range(count)]) for t in range(1, count)]


def on_device(vectors, col_blocks, op_ids, coefficients, onsite, phonon_ops):
    vec_count, row_count = vectors.shape
    op_count, block_size = phonon_ops.shape[0], phonon_ops.shape[1]
    per_row = col_blocks.shape[1]
    block_count = row_count // block_size
    parts = lax.axis_size("vec")
    row_axis = lax.axis_size("row")
    bands = block_count // BAND
    if parts <= 8 and bands % 16 == 0 and (bands // 16 * BAND) % parts == 0:
        unit = bands // 16
        low_group, middle, high_group = (0, 2 * unit), (2 * unit, 8 * unit), (10 * unit, 6 * unit)
        order = [middle, high_group, low_group]
    else:
        order = [(0, bands)]
    me = lax.axis_index("vec").astype(jnp.int32)[None]
    first_block = lax.axis_index("row") * block_count
    upward = [(i, i + 1) for i in range(row_axis - 1)]
    downward = [(i + 1, i) for i in range(row_axis - 1)]

    def index_of(code):
        column = jnp.maximum(code // op_count - first_block + 2 * BAND, 0)
        return column % (RING * BAND) * op_count + code % op_count

    def with_ends(low_part, middle, high_part):
        return jnp.concatenate([low_part, middle, high_part])

    code = (col_blocks * op_count + op_ids).reshape(-1)
    coef = coefficients.reshape(-1)
    tail = BAND * per_row
    no_rows = jnp.zeros((tail,), jnp.int32)
    no_site = jnp.zeros((tail,), jnp.float32)
    inner = (
        index_of(with_ends(no_rows, code, no_rows)),
        with_ends(no_site, coef, no_site),
        onsite[None, :],
    )

    w_op = jnp.transpose(phonon_ops, (2, 0, 1)).reshape(block_size, op_count * block_size)
    w_high = lax.reduce_precision(w_op, 8, 7)
    w = jnp.concatenate([w_high, w_high, w_op - w_high], axis=0).astype(jnp.bfloat16)

    def first(table, start, count, low=None, high=None):
        return apply_ham(
            me, *table, w, vectors, max(start - 2, 0), count, start, start, start - 1 if table is inner else start,
            low=low, high=high, op_count=op_count, per_row=per_row,
        )[0]

    def second(group, main, main_chunk, **kwargs):
        start, count = group
        part_blocks = count * BAND // parts
        return apply_ham(
            me, *inner, w, main, main_chunk, count, start + 1, start + 1, start,
            base=vectors, base_chunk=start, parts=parts, part_blocks=part_blocks, op_count=op_count, per_row=per_row, **kwargs,
        )

    received = {}
    halo = 2 * BAND * block_size
    end_size = 2 * tail + BAND * block_size
    end_width = -(-end_size // (vec_count * LANES)) * LANES
    edges = []
    for a, b, c, d, e, f in (
        (code.shape[0] - tail, code.shape[0], row_count - BAND * block_size, row_count, row_count - halo, row_count),
        (0, tail, 0, BAND * block_size, 0, halo),
    ):
        end = jnp.concatenate([code[a:b].astype(jnp.float32), coef[a:b], onsite[c:d]])
        end = jnp.pad(end, (0, vec_count * end_width - end_size)).reshape(vec_count, end_width)
        edges.append(jnp.concatenate([vectors[:, e:f], end], axis=1))
    if len(order) > 1:
        step_mid = first(inner, middle[0], middle[1] + 2)
        step_mid, edges = lax.optimization_barrier((step_mid, edges))
    low_vectors = lax.ppermute(edges[0], "row", upward)
    high_vectors = lax.ppermute(edges[1], "row", downward)
    low_end = low_vectors[:, halo:].reshape(-1)[:end_size]
    high_end = high_vectors[:, halo:].reshape(-1)[:end_size]
    outer = (
        index_of(with_ends(low_end[:tail].astype(jnp.int32), code, high_end[:tail].astype(jnp.int32))),
        with_ends(low_end[tail : 2 * tail], coef, high_end[tail : 2 * tail]),
        with_ends(low_end[2 * tail :], onsite, high_end[2 * tail :])[None, :],
    )
    if len(order) == 1:
        steps = first(outer, 0, bands + 2, low=low_vectors, high=high_vectors)
        received[order[0]] = exchange(second(order[0], steps, 0), "vec")
    else:
        received[middle] = exchange(second(middle, step_mid, 0), "vec")
        step_high = first(outer, high_group[0] + 2, high_group[1], high=high_vectors)
        received[high_group] = exchange(
            second(high_group, step_high, 0, low=step_mid, low_chunk=middle[1]), "vec"
        )
        step_low = first(outer, 0, low_group[1], low=low_vectors)
        received[low_group] = exchange(second(low_group, step_low, 0, high=step_mid, high_chunk=0), "vec")

    stacks = {}
    before = None
    for batch in (order[:-1], order[-1:]):
        if batch:
            out = gram_step(me, [received[group] for group in batch], before, batch[-1] == order[-1])
            for number, group in enumerate(batch):
                stacks[group] = out[2 * number : 2 * number + 2]
            out = out[2 * len(batch) :]
            before = out[0]
    mine = sum_of(exchange(out, "vec"))
    summed = sum_of(
        [mine] + [lax.ppermute(mine, "row", [(i, i ^ k) for i in range(row_axis)]) for k in range(1, row_axis)]
    )
    shares = [summed] + [
        lax.ppermute(summed, "vec", [(i, i ^ t) for i in range(parts)]) for t in range(1, parts)
    ]
    rot_hi, rot_lo = inverse_of(me, shares, vec_count * parts, float(row_count * row_axis))

    result = None
    for group in order:
        stride = group[1] * BAND * block_size // parts
        cuts = 2 if group != order[-1] else 1
        for cut in range(cuts):
            pieces = exchange(rotate_step(me, rot_hi, rot_lo, *stacks[group], parts, cut, cuts), "vec")
            offset = group[0] * BAND * block_size + cut * (stride // cuts)
            result = place_step(me, pieces, result, offset, stride, vectors.shape)
    return result


def solution(mesh):
    return jax.shard_map(
        on_device,
        mesh=mesh,
        in_specs=(P("vec", "row"), P("row", None), P("row", None), P("row", None), P("row"), P()),
        out_specs=P("vec", "row"),
        check_vma=False,
    )
```
